1024 devices in a mesh: grp: 4 (over z_hi, core), lat: 8 (over z_lo), lon: 32 (over y, x).
Axes of the slice: x: 4, y: 8, z: 16 (z_hi: 2, z_lo: 8; z = z_hi * 8 + z_lo), core: 2. Of those that a mesh axis runs over, the one named last changes fastest.
Arguments:
- state: float32 [5, 128, 256, 512], P(None, 'lon', 'lat', 'grp'), may hold values from -5 to 5
- tracers: float32 [12, 256, 512, 128], P(None, 'lat', ('grp', 'lon')), may hold values from 0.1 to 1.5
- coupling: float32 [5, 5], replicated, may hold values from -0.8 to 0.8
- rates: float32 [24], replicated, may hold values from 0.05 to 0.5
- pairs: int32 [24, 3], replicated, may hold values from 0 to 11
- heat_map: int32 [12], replicated, may hold values from 0 to 3
- heat_coef: float32 [4], replicated, may hold values from 0.5 to 2
Outputs:
- state_out: float32 [5, 128, 256, 512], P(None, 'lon', 'lat', 'grp')
- tracers_out: float32 [12, 256, 512, 128], P(None, 'lat', ('grp', 'lon'))
The draws below stay inside these ranges and needn't reach their ends.
All inputs are finite; a program needn't handle non-finite values.
Results may differ from the reference program's by a relative error of at most 0.000052.
Values sent between devices are 32-bit elements; how exact they have to be, the bound alone decides.
No kernel may reach another device: no remote copies, remote signals or barrier semaphores. Data moves between devices by JAX's collectives and lax.ppermute only.
A program may use at most 32 MiB of HBM per device.

```python
import math
import jax
import jax.numpy as jnp
from jax import lax

NF = 5
NT = 12
NR = 24
NH = 4
NX = 256
NY = 512
NZ = 128


def set_ends(values, rng, low, high):
    longest = values.shape.index(max(values.shape))
    spots = []
    for shift in (0, 1):
        where = [jax.random.randint(jax.random.fold_in(rng, axis), (), 0, length) for axis, length in enumerate(values.shape)]
        where[longest] = (where[longest] + shift) % values.shape[longest]
        spots.append(tuple(where))
    return values.at[spots[0]].set(low).at[spots[1]].set(high)


def level_of(own_key, extent, pieces, smallest, high):
    gain, own = 1.0, jax.random.fold_in(own_key, 6)
    for axis_at, blocks in pieces:
        draws = jnp.exp(jax.random.uniform(jax.random.fold_in(own, axis_at), (blocks,), jnp.float32, smallest / len(pieces), high / len(pieces)))
        gain = gain * jnp.repeat(draws, extent[axis_at] // blocks).reshape([-1 if axis == axis_at else 1 for axis in range(len(extent))])
    return gain


def gaussian(own_key, shape, spread, bound, shards=(), kind=jnp.bfloat16):
    array = spread * jax.random.normal(own_key, shape, jnp.float32)
    if shards:
        array = array * level_of(own_key, shape, shards, -0.22, 0.18)
    return jnp.clip(array, -bound, bound).astype(kind)


def setup_inputs(seed: int = 0) -> dict:
    keys = jax.random.split(jax.random.key(seed), 8)
    return {
        "state": gaussian(keys[0], (NF, NZ, NX, NY), 1.0, 5.0, ((1, 32), (2, 8), (3, 4)), jnp.float32),
        "tracers": jnp.clip(jnp.exp(math.log(1.5) - 2.7080502 * jax.random.uniform(keys[1], (NT, NX, NY, NZ), jnp.float32) ** level_of(keys[1], (NT, NX, NY, NZ), ((1, 8), (2, 128)), -0.2, 0.2)), 0.1, 1.5),
        "coupling": gaussian(keys[2], (NF, NF), 0.2, 0.8, (), jnp.float32),
        "rates": jnp.clip(jnp.exp(jax.random.uniform(keys[3], (NR,), jnp.float32, math.log(0.05), math.log(0.5))), 0.05, 0.5),
        "pairs": set_ends(jax.random.randint(keys[4], (NR, 3), 0, NT), jax.random.fold_in(keys[4], 1), 0, NT - 1).astype(jnp.int32),
        "heat_map": set_ends(jax.random.randint(keys[5], (NT,), 0, NH), jax.random.fold_in(keys[5], 1), 0, NH - 1).astype(jnp.int32),
        "heat_coef": jnp.clip(jax.random.uniform(keys[6], (NH,), jnp.float32, 0.5, 2.0), 0.5, 2.0),
    }


HIGH = lax.Precision.HIGHEST


def neighbour(field, offset, axis, periodic):
    if periodic:
        return jnp.roll(field, -offset, axis)
    length = field.shape[axis]
    zeros = jnp.zeros_like(lax.slice_in_dim(field, 0, abs(offset), axis=axis))
    if offset > 0:
        return jnp.concatenate([lax.slice_in_dim(field, offset, length, axis=axis), zeros], axis)
    return jnp.concatenate([zeros, lax.slice_in_dim(field, 0, length + offset, axis=axis)], axis)


def stencil(center, plus_one, plus_two, minus_one, minus_two):
    advect = -(8.0 * (plus_one - minus_one) - (plus_two - minus_two)) * (0.3 / 12.0)
    return advect + 0.1 * (plus_one + minus_one - 2.0 * center)


def tendency(fields, coupling):
    along_x = stencil(fields, neighbour(fields, 1, 2, False), neighbour(fields, 2, 2, False),
                      neighbour(fields, -1, 2, False), neighbour(fields, -2, 2, False))
    along_y = stencil(fields, neighbour(fields, 1, 3, True), neighbour(fields, 2, 3, True),
                      neighbour(fields, -1, 3, True), neighbour(fields, -2, 3, True))
    mixed = jnp.einsum("fg,gzxy->fzxy", coupling, fields, precision=HIGH)
    return along_x + along_y + mixed


def clamped(field, axis):
    length = field.shape[axis]
    higher = jnp.concatenate([lax.slice_in_dim(field, 1, length, axis=axis),
                              lax.slice_in_dim(field, length - 1, length, axis=axis)], axis)
    lower = jnp.concatenate([lax.slice_in_dim(field, 0, 1, axis=axis),
                             lax.slice_in_dim(field, 0, length - 1, axis=axis)], axis)
    return higher, lower


def mixing_of(east_diff, north_diff):
    shear = east_diff * east_diff + north_diff * north_diff
    return 0.2 * shear / (1.0 + shear)


def column_step(species, mixing_k, vertical, rates, pairs, heat_map, heat_coef):
    speed = 0.4 * vertical / (1.0 + jnp.abs(vertical))
    rising = jnp.maximum(speed, 0.0)
    sinking = jnp.minimum(speed, 0.0)
    higher, lower = clamped(species, 2)
    advect = -rising * (species - lower) - sinking * (higher - species)
    diffuse = mixing_k * (higher - 2.0 * species + lower)
    flat = species.reshape(species.shape[0], -1)
    labels = jnp.arange(species.shape[0], dtype=jnp.int32)
    first = (pairs[:, 0:1] == labels[None, :]).astype(jnp.float32)
    second = (pairs[:, 1:2] == labels[None, :]).astype(jnp.float32)
    product = (pairs[:, 2:3] == labels[None, :]).astype(jnp.float32)
    conc_a = jnp.dot(first, flat, precision=HIGH)
    conc_b = jnp.dot(second, flat, precision=HIGH)
    reaction = rates[:, None] * conc_a * conc_b
    stoich = product - first - second
    change = jnp.dot(stoich.T, reaction, precision=HIGH)
    classes = jnp.arange(heat_coef.shape[0], dtype=jnp.int32)
    weights = jnp.dot((heat_map[:, None] == classes[None, :]).astype(jnp.float32), heat_coef, precision=HIGH)
    heat = jnp.dot(weights, change, precision=HIGH)
    renewed = species + advect + diffuse + change.reshape(species.shape)
    return renewed, heat.reshape(mixing_k.shape)


def runge_kutta(state, coupling):
    section_one = state + tendency(state, coupling)
    section_two = 0.75 * state + 0.25 * (section_one + tendency(section_one, coupling))
    return state / 3.0 + (2.0 / 3.0) * (section_two + tendency(section_two, coupling))


def reference(state, tracers, coupling, rates, pairs, heat_map, heat_coef):
    stepped = runge_kutta(state, coupling)

    def one_row(items):
        species, winds = items
        winds = jnp.transpose(winds, (0, 2, 1))
        higher, lower = clamped(winds[0:2], 2)
        diffs = higher - lower
        mixing_k = mixing_of(diffs[0], diffs[1])
        return column_step(species, mixing_k, winds[2], rates, pairs, heat_map, heat_coef)

    new_rows, heat_rows = lax.map(one_row, (jnp.moveaxis(tracers, 1, 0), jnp.moveaxis(stepped[0:3], 2, 0)))
    tracers_out = jnp.moveaxis(new_rows, 0, 1)
    heat = jnp.transpose(heat_rows, (2, 0, 1))
    state_out = stepped.at[3].set(stepped[3] + 0.5 * heat)
    return state_out, tracers_out
```

```python
import jax
import jax.numpy as jnp
from jax import lax
from jax.experimental import pallas as pl
from jax.experimental.pallas import tpu as pltpu
from jax.sharding import PartitionSpec as P

FIELDS = 5
LEVELS = 4
PLANES = FIELDS * LEVELS
ROWS = 32
LANES = 128
HALO = 6
BAND = 8
PEERS = 32
SLOTS = 16
SPECIES = 12
REACTIONS = 24


def lane_index(rows):
    return lax.broadcasted_iota(jnp.int32, (rows, LANES), 1)


def pack_kernel(state_ref, far_ref, near_ref):
    odd = lax.rem(lax.axis_index("grp"), 2) == 1
    lanes = lane_index(ROWS)
    left = jnp.zeros((ROWS, LANES), jnp.float32)
    right = jnp.zeros((ROWS, LANES), jnp.float32)
    for plane in range(PLANES):
        tile = state_ref[plane]
        keep = lanes >= HALO * plane
        left = jnp.where(keep, pltpu.roll(tile, HALO * plane, 1) if plane else tile, left)
        right = jnp.where(keep, pltpu.roll(tile, HALO * plane + HALO, 1), right)
    far_ref[...] = jnp.where(odd, right, left)
    near_ref[...] = jnp.where(odd, left, right)


def regroup(chunks):
    lanes = lane_index(ROWS)
    width = LANES // 4
    out = []
    for j in range(4):
        total = None
        for i in range(4):
            turn = (width * (i - j)) % LANES
            moved = pltpu.roll(chunks[i], turn, 1) if turn else chunks[i]
            total = moved if total is None else jnp.where(lanes >= width * i, moved, total)
        out.append(total)
    return out


def chem_kernel(rates_ref, pairs_ref, map_ref, coef_ref, q_ref, pre_ref, heat_ref, heat_sc, turn_sc):
    pre_ref[...] = q_ref[...]
    heat_sc[...] = jnp.zeros_like(heat_sc)

    def weight(species):
        return coef_ref[map_ref[species]]

    def react(r, carry):
        a, b, p = pairs_ref[r, 0], pairs_ref[r, 1], pairs_ref[r, 2]
        rate = rates_ref[r] * q_ref[a] * q_ref[b]
        heat_sc[...] += (weight(p) - weight(a) - weight(b)) * rate
        pre_ref[p] += rate
        pre_ref[a] -= rate
        pre_ref[b] -= rate
        return carry

    lax.fori_loop(0, REACTIONS, react, 0)
    ordered = jnp.concatenate([heat_sc[pl.ds(y, ROWS, stride=4), :] for y in range(4)], 0)
    turn_sc[...] = jnp.transpose(ordered)
    chunks = [turn_sc[pl.ds(level, PEERS, stride=4), :] for level in range(4)]
    for y, block in enumerate(regroup(chunks)):
        heat_ref[y] = block


def rk_kernel(
    coupling_ref, state_ref, low_ref, high_ref, far_ref, near_ref, under_ref, over_ref, heat_ref,
    out_ref, send_ref, sa, sb, ta, tb, ua, ub, turn_sc,
):
    odd = lax.rem(lax.axis_index("grp"), 2) == 1
    lat = lax.axis_index("lat")
    has_low = lat > 0
    has_high = lat < lax.axis_size("lat") - 1
    base = 16

    far = jnp.concatenate([under_ref[0:BAND], far_ref[...], over_ref[0:BAND]], 0)
    near = jnp.concatenate([under_ref[BAND:], near_ref[...], over_ref[BAND:]], 0)
    left = jnp.where(odd, near, far)
    right = jnp.where(odd, far, near)
    span = ROWS + 2 * BAND
    lanes = lane_index(span)
    for plane in range(PLANES):
        sa[plane, base - BAND : base, :] = low_ref[plane]
        sa[plane, base : base + ROWS, :] = state_ref[plane]
        sa[plane, base + ROWS : base + ROWS + BAND, :] = high_ref[plane]
        beyond = pltpu.roll(right, (-HALO * plane) % LANES, 1) if plane else right
        before = pltpu.roll(left, (LANES - HALO - HALO * plane) % LANES, 1)
        edge = jnp.where(lanes >= LANES - HALO, before, 0.0)
        sb[plane, base - BAND : base + ROWS + BAND, :] = jnp.where(lanes < HALO, beyond, edge)

    lane8 = lane_index(8)
    weights = [
        [coupling_ref[f, g] + (0.6 if f == g else 0.0) for g in range(FIELDS)] for f in range(FIELDS)
    ]

    def apply(a_ref, b_ref, z, row, both):
        centers_a = [a_ref[f * LEVELS + z, row : row + 8, :] for f in range(FIELDS)]
        centers_b = [b_ref[f * LEVELS + z, row : row + 8, :] for f in range(FIELDS)]

        def along_lanes(f):
            moved = {}
            for j in (1, 2, -1, -2):
                ra = pltpu.roll(centers_a[f], -j % LANES, 1)
                rb = pltpu.roll(centers_b[f], -j % LANES, 1)
                inner = lane8 < LANES - j if j > 0 else lane8 >= -j
                moved[j] = (jnp.where(inner, ra, rb), jnp.where(inner, rb, ra) if both else None)
            return moved

        result = []
        for f in range(FIELDS):
            moved = along_lanes(f)
            pieces = []
            for part, ref, centers in ((0, a_ref, centers_a), (1, b_ref, centers_b)):
                if part == 1 and not both:
                    break
                x = {j: ref[f * LEVELS + z, row + j : row + j + 8, :] for j in (1, 2, -1, -2)}
                total = -0.1 * (x[1] + moved[1][part]) + 0.3 * (x[-1] + moved[-1][part])
                total = total + 0.025 * ((x[2] - x[-2]) + (moved[2][part] - moved[-2][part]))
                for g in range(FIELDS):
                    total = total + weights[f][g] * centers[g]
                pieces.append(total)
            result.append(pieces)
        return result

    first, last = base - BAND, base + ROWS

    def masked(value, row):
        if row == first:
            return jnp.where(has_low, value, 0.0)
        if row == last:
            return jnp.where(has_high, value, 0.0)
        return value

    def stage_one(z, carry):
        for row in range(first, last + 8, 8):
            for f, (a, b) in enumerate(apply(sa, sb, z, row, True)):
                ta[f * LEVELS + z, row : row + 8, :] = masked(a, row)
                tb[f * LEVELS + z, row : row + 8, :] = masked(b, row)
        return carry

    def stage_two(z, carry):
        for row in range(first, last + 8, 8):
            for f, (a, b) in enumerate(apply(ta, tb, z, row, True)):
                plane = f * LEVELS + z
                ua[plane, row : row + 8, :] = masked(0.75 * sa[plane, row : row + 8, :] + 0.25 * a, row)
                ub[plane, row : row + 8, :] = masked(0.75 * sb[plane, row : row + 8, :] + 0.25 * b, row)
        return carry

    def stage_three(z, carry):
        for row in range(base, last, 8):
            for f, (a,) in enumerate(apply(ua, ub, z, row, False)):
                plane = f * LEVELS + z
                value = sa[plane, row : row + 8, :] * (1.0 / 3.0) + (2.0 / 3.0) * a
                out_ref[plane, row - base : row - base + 8, :] = value
        return carry

    lax.fori_loop(0, LEVELS, stage_one, 0)
    lax.fori_loop(0, LEVELS, stage_two, 0)
    lax.fori_loop(0, LEVELS, stage_three, 0)

    for f in range(3):
        plane = jnp.concatenate([out_ref[f * LEVELS + z] for z in range(LEVELS)], 0)
        turn_sc[f] = jnp.transpose(plane)
        chunks = [turn_sc[f, pl.ds(y, PEERS, stride=4), :] for y in range(4)]
        for level, block in enumerate(regroup(chunks)):
            send_ref[pl.ds(4 * f + level, PEERS, stride=SLOTS), :] = block
    for y in range(4):
        send_ref[pl.ds(12 + y, PEERS, stride=SLOTS), :] = heat_ref[y]


def final_kernel(recv_ref, temp_ref, q_ref, pre_ref, temp_out_ref, q_out_ref, turn_sc, wind_sc):
    for y in range(4):
        turn_sc[pl.ds(y, PEERS, stride=4), :] = recv_ref[pl.ds(12 + y, PEERS, stride=SLOTS), :]
    temp_out_ref[0] = temp_ref[0] + 0.5 * jnp.transpose(turn_sc[...])
    for f in range(3):
        for level in range(4):
            turn_sc[pl.ds(level, PEERS, stride=4), :] = recv_ref[pl.ds(4 * f + level, PEERS, stride=SLOTS), :]
        columns = jnp.transpose(turn_sc[...])
        for y in range(4):
            wind_sc[f, pl.ds(y, ROWS, stride=4), :] = columns[y * ROWS : (y + 1) * ROWS]

    chunk = 32
    lanes = lane_index(chunk)

    def clamped(value):
        higher = jnp.where(lanes == LANES - 1, value, pltpu.roll(value, LANES - 1, 1))
        lower = jnp.where(lanes == 0, value, pltpu.roll(value, 1, 1))
        return higher, lower

    for start in range(0, 128, chunk):
        rows = slice(start, start + chunk)
        shear = None
        for f in range(2):
            higher, lower = clamped(wind_sc[f, rows, :])
            square = (higher - lower) * (higher - lower)
            shear = square if shear is None else shear + square
        mixing = 0.2 * shear / (1.0 + shear)
        vertical = wind_sc[2, rows, :]
        speed = 0.4 * vertical / (1.0 + jnp.abs(vertical))
        up = mixing - jnp.minimum(speed, 0.0)
        down = mixing + jnp.maximum(speed, 0.0)
        for s in range(SPECIES):
            value = q_ref[s, rows, :]
            higher, lower = clamped(value)
            q_out_ref[s, rows, :] = pre_ref[s, rows, :] + (up * (higher - value) - down * (value - lower))


VMEM = pl.BlockSpec(memory_space=pltpu.VMEM)
SMEM = pl.BlockSpec(memory_space=pltpu.SMEM)


def shape(*dims):
    return jax.ShapeDtypeStruct(dims, jnp.float32)


def cost(flops, data):
    return pl.CostEstimate(flops=flops, bytes_accessed=data, transcendentals=0)


def on_device(state, tracers, coupling, rates, pairs, heat_map, heat_coef):
    planes = state.reshape(PLANES, ROWS, LANES)
    q = tracers.reshape(SPECIES, 128, 128)

    far, near = pl.pallas_call(
        pack_kernel,
        out_shape=(shape(ROWS, LANES), shape(ROWS, LANES)),
        in_specs=[VMEM],
        out_specs=(VMEM, VMEM),
        cost_estimate=cost(1000000, 400000),
    )(planes)
    far_in = lax.ppermute(far, "grp", [(0, 3), (3, 0), (1, 2), (2, 1)])
    near_in = lax.ppermute(near, "grp", [(0, 1), (1, 0), (2, 3), (3, 2)])
    count = lax.axis_size("lat")
    up = [(i, i + 1) for i in range(count - 1)]
    down = [(i + 1, i) for i in range(count - 1)]
    low = lax.ppermute(planes[:, ROWS - BAND :], "lat", up)
    high = lax.ppermute(planes[:, :BAND], "lat", down)

    pre, heat = pl.pallas_call(
        chem_kernel,
        out_shape=(shape(SPECIES, 128, 128), shape(4, PEERS, LANES)),
        in_specs=[SMEM, SMEM, SMEM, SMEM, VMEM],
        out_specs=(VMEM, VMEM),
        scratch_shapes=[pltpu.VMEM((128, 128), jnp.float32), pltpu.VMEM((128, 128), jnp.float32)],
        cost_estimate=cost(10000000, 2000000),
    )(rates, pairs, heat_map, heat_coef, q)

    under = lax.ppermute(jnp.concatenate([far_in[ROWS - BAND :], near_in[ROWS - BAND :]], 0), "lat", up)
    over = lax.ppermute(jnp.concatenate([far_in[:BAND], near_in[:BAND]], 0), "lat", down)

    extended = pltpu.VMEM((PLANES, 64, LANES), jnp.float32)
    stepped, send = pl.pallas_call(
        rk_kernel,
        out_shape=(shape(PLANES, ROWS, LANES), shape(PEERS * SLOTS, LANES)),
        in_specs=[SMEM] + [VMEM] * 8,
        out_specs=(VMEM, VMEM),
        scratch_shapes=[extended] * 6 + [pltpu.VMEM((3, 128, 128), jnp.float32)],
        cost_estimate=cost(20000000, 1500000),
    )(coupling, planes, low, high, far_in, near_in, under, over, heat)

    received = lax.all_to_all(
        send.reshape(PEERS, SLOTS, LANES), "lon", split_axis=0, concat_axis=0, tiled=True
    )
    temperature = pl.BlockSpec((1, 128, 128), lambda i: (3, 0, 0))
    whole = pl.BlockSpec((SPECIES, 128, 128), lambda i: (0, 0, 0))
    state_out, q_out = pl.pallas_call(
        final_kernel,
        grid=(1,),
        out_shape=(shape(FIELDS, 128, 128), shape(SPECIES, 128, 128)),
        in_specs=[pl.BlockSpec((PEERS * SLOTS, LANES), lambda i: (0, 0)), temperature, whole, whole],
        out_specs=(temperature, whole),
        scratch_shapes=[pltpu.VMEM((128, 128), jnp.float32), pltpu.VMEM((3, 128, 128), jnp.float32)],
        input_output_aliases={1: 0},
        cost_estimate=cost(10000000, 2500000),
    )(received.reshape(PEERS * SLOTS, LANES), stepped.reshape(FIELDS, 128, 128), q, pre)
    return state_out.reshape(state.shape), q_out.reshape(tracers.shape)


def solution(mesh):
    in_specs = (
        P(None, "lon", "lat", "grp"),
        P(None, "lat", ("grp", "lon"), None),
        P(),
        P(),
        P(),
        P(),
        P(),
    )
    out_specs = (P(None, "lon", "lat", "grp"), P(None, "lat", ("grp", "lon"), None))
    return jax.shard_map(
        on_device, mesh=mesh, in_specs=in_specs, out_specs=out_specs, check_vma=False
    )
```

```python
import jax
import jax.numpy as jnp
from jax import lax
from jax.experimental import pallas as pl
from jax.experimental.pallas import tpu as pltpu
from jax.sharding import PartitionSpec as P

FIELDS = 5
LEVELS = 4
PLANES = FIELDS * LEVELS
ROWS = 32
LANES = 128
HALO = 6
BAND = 8
SPAN = ROWS + 2 * BAND
PEERS = 32
SLOTS = 16
SPECIES = 12
REACTIONS = 24


def lane_index(rows):
    return lax.broadcasted_iota(jnp.int32, (rows, LANES), 1)


def pack_kernel(state_ref, low_ref, high_ref, far_ref, near_ref):
    odd = lax.rem(lax.axis_index("grp"), 2) == 1
    for source, rows, start in ((low_ref, BAND, 0), (state_ref, ROWS, BAND), (high_ref, BAND, BAND + ROWS)):
        lanes = lane_index(rows)
        left = source[0]
        right = pltpu.roll(source[0], HALO, 1)
        for plane in range(1, PLANES):
            keep = lanes >= HALO * plane
            left = jnp.where(keep, pltpu.roll(source[plane], HALO * plane, 1), left)
            right = jnp.where(keep, pltpu.roll(source[plane], HALO * plane + HALO, 1), right)
        far_ref[start : start + rows] = jnp.where(odd, right, left)
        near_ref[start : start + rows] = jnp.where(odd, left, right)


def regroup(chunks):
    lanes = lane_index(ROWS)
    width = LANES // 4
    out = []
    for j in range(4):
        total = None
        for i in range(4):
            turn = (width * (i - j)) % LANES
            moved = pltpu.roll(chunks[i], turn, 1) if turn else chunks[i]
            total = moved if total is None else jnp.where(lanes >= width * i, moved, total)
        out.append(total)
    return out


def chem_kernel(rates_ref, pairs_ref, map_ref, coef_ref, q_ref, pre_ref, heat_ref, heat_sc, turn_sc):
    pre_ref[...] = q_ref[...]
    heat_sc[...] = jnp.zeros_like(heat_sc)

    def weight(species):
        return coef_ref[map_ref[species]]

    def react(r, carry):
        a, b, p = pairs_ref[r, 0], pairs_ref[r, 1], pairs_ref[r, 2]
        rate = rates_ref[r] * q_ref[a] * q_ref[b]
        heat_sc[...] += (weight(p) - weight(a) - weight(b)) * rate
        pre_ref[p] += rate
        pre_ref[a] -= rate
        pre_ref[b] -= rate
        return carry

    lax.fori_loop(0, REACTIONS, react, 0)
    ordered = jnp.concatenate([heat_sc[pl.ds(y, ROWS, stride=4), :] for y in range(4)], 0)
    turn_sc[...] = jnp.transpose(ordered)
    chunks = [turn_sc[pl.ds(level, PEERS, stride=4), :] for level in range(4)]
    for y, block in enumerate(regroup(chunks)):
        heat_ref[y] = block


def rk_kernel(
    coupling_ref, state_ref, low_ref, high_ref, far_ref, near_ref, heat_ref,
    out_ref, send_ref, sa, sb, ta, tb, ua, ub, turn_sc,
):
    odd = lax.rem(lax.axis_index("grp"), 2) == 1
    lat = lax.axis_index("lat")
    has_low = lat > 0
    has_high = lat < lax.axis_size("lat") - 1
    base = 16

    left = jnp.where(odd, near_ref[...], far_ref[...])
    right = jnp.where(odd, far_ref[...], near_ref[...])
    lanes = lane_index(SPAN)
    for plane in range(PLANES):
        sa[plane, base - BAND : base, :] = low_ref[plane]
        sa[plane, base : base + ROWS, :] = state_ref[plane]
        sa[plane, base + ROWS : base + ROWS + BAND, :] = high_ref[plane]
        beyond = pltpu.roll(right, (-HALO * plane) % LANES, 1) if plane else right
        before = pltpu.roll(left, (LANES - HALO - HALO * plane) % LANES, 1)
        edge = jnp.where(lanes >= LANES - HALO, before, 0.0)
        sb[plane, base - BAND : base + ROWS + BAND, :] = jnp.where(lanes < HALO, beyond, edge)

    lane8 = lane_index(8)
    weights = [
        [coupling_ref[f, g] + (0.6 if f == g else 0.0) for g in range(FIELDS)] for f in range(FIELDS)
    ]

    def apply(a_ref, b_ref, z, row, both):
        centers_a = [a_ref[f * LEVELS + z, row : row + 8, :] for f in range(FIELDS)]
        centers_b = [b_ref[f * LEVELS + z, row : row + 8, :] for f in range(FIELDS)]

        def along_lanes(f):
            moved = {}
            for j in (1, 2, -1, -2):
                ra = pltpu.roll(centers_a[f], -j % LANES, 1)
                rb = pltpu.roll(centers_b[f], -j % LANES, 1)
                inner = lane8 < LANES - j if j > 0 else lane8 >= -j
                moved[j] = (jnp.where(inner, ra, rb), jnp.where(inner, rb, ra) if both else None)
            return moved

        result = []
        for f in range(FIELDS):
            moved = along_lanes(f)
            pieces = []
            for part, ref, centers in ((0, a_ref, centers_a), (1, b_ref, centers_b)):
                if part == 1 and not both:
                    break
                x = {j: ref[f * LEVELS + z, row + j : row + j + 8, :] for j in (1, 2, -1, -2)}
                total = -0.1 * (x[1] + moved[1][part]) + 0.3 * (x[-1] + moved[-1][part])
                total = total + 0.025 * ((x[2] - x[-2]) + (moved[2][part] - moved[-2][part]))
                for g in range(FIELDS):
                    total = total + weights[f][g] * centers[g]
                pieces.append(total)
            result.append(pieces)
        return result

    first, last = base - BAND, base + ROWS

    def masked(value, row):
        if row == first:
            return jnp.where(has_low, value, 0.0)
        if row == last:
            return jnp.where(has_high, value, 0.0)
        return value

    def stage_one(z, carry):
        for row in range(first, last + 8, 8):
            for f, (a, b) in enumerate(apply(sa, sb, z, row, True)):
                ta[f * LEVELS + z, row : row + 8, :] = masked(a, row)
                tb[f * LEVELS + z, row : row + 8, :] = masked(b, row)
        return carry

    def stage_two(z, carry):
        for row in range(first, last + 8, 8):
            for f, (a, b) in enumerate(apply(ta, tb, z, row, True)):
                plane = f * LEVELS + z
                ua[plane, row : row + 8, :] = masked(0.75 * sa[plane, row : row + 8, :] + 0.25 * a, row)
                ub[plane, row : row + 8, :] = masked(0.75 * sb[plane, row : row + 8, :] + 0.25 * b, row)
        return carry

    def stage_three(z, carry):
        for row in range(base, last, 8):
            for f, (a,) in enumerate(apply(ua, ub, z, row, False)):
                plane = f * LEVELS + z
                value = sa[plane, row : row + 8, :] * (1.0 / 3.0) + (2.0 / 3.0) * a
                out_ref[plane, row - base : row - base + 8, :] = value
        return carry

    lax.fori_loop(0, LEVELS, stage_one, 0)
    lax.fori_loop(0, LEVELS, stage_two, 0)
    lax.fori_loop(0, LEVELS, stage_three, 0)

    for f in range(3):
        plane = jnp.concatenate([out_ref[f * LEVELS + z] for z in range(LEVELS)], 0)
        turn_sc[f] = jnp.transpose(plane)
        chunks = [turn_sc[f, pl.ds(y, PEERS, stride=4), :] for y in range(4)]
        for level, block in enumerate(regroup(chunks)):
            send_ref[pl.ds(4 * f + level, PEERS, stride=SLOTS), :] = block
    for y in range(4):
        send_ref[pl.ds(12 + y, PEERS, stride=SLOTS), :] = heat_ref[y]


def final_kernel(recv_ref, temp_ref, q_ref, pre_ref, temp_out_ref, q_out_ref, turn_sc, wind_sc):
    for y in range(4):
        turn_sc[pl.ds(y, PEERS, stride=4), :] = recv_ref[pl.ds(12 + y, PEERS, stride=SLOTS), :]
    temp_out_ref[0] = temp_ref[0] + 0.5 * jnp.transpose(turn_sc[...])
    for f in range(3):
        for level in range(4):
            turn_sc[pl.ds(level, PEERS, stride=4), :] = recv_ref[pl.ds(4 * f + level, PEERS, stride=SLOTS), :]
        columns = jnp.transpose(turn_sc[...])
        for y in range(4):
            wind_sc[f, pl.ds(y, ROWS, stride=4), :] = columns[y * ROWS : (y + 1) * ROWS]

    chunk = 32
    lanes = lane_index(chunk)

    def clamped(value):
        higher = jnp.where(lanes == LANES - 1, value, pltpu.roll(value, LANES - 1, 1))
        lower = jnp.where(lanes == 0, value, pltpu.roll(value, 1, 1))
        return higher, lower

    for start in range(0, 128, chunk):
        rows = slice(start, start + chunk)
        shear = None
        for f in range(2):
            higher, lower = clamped(wind_sc[f, rows, :])
            square = (higher - lower) * (higher - lower)
            shear = square if shear is None else shear + square
        mixing = 0.2 * shear / (1.0 + shear)
        vertical = wind_sc[2, rows, :]
        speed = 0.4 * vertical / (1.0 + jnp.abs(vertical))
        up = mixing - jnp.minimum(speed, 0.0)
        down = mixing + jnp.maximum(speed, 0.0)
        for s in range(SPECIES):
            value = q_ref[s, rows, :]
            higher, lower = clamped(value)
            q_out_ref[s, rows, :] = pre_ref[s, rows, :] + (up * (higher - value) - down * (value - lower))


VMEM = pl.BlockSpec(memory_space=pltpu.VMEM)
SMEM = pl.BlockSpec(memory_space=pltpu.SMEM)
PARAMS = pltpu.CompilerParams(vmem_limit_bytes=16 * 1024 * 1024)


def shape(*dims):
    return jax.ShapeDtypeStruct(dims, jnp.float32)


def cost(flops, data):
    return pl.CostEstimate(flops=flops, bytes_accessed=data, transcendentals=0)


def on_device(state, tracers, coupling, rates, pairs, heat_map, heat_coef):
    planes = state.reshape(PLANES, ROWS, LANES)
    q = tracers.reshape(SPECIES, 128, 128)

    count = lax.axis_size("lat")
    low = lax.ppermute(planes[:, ROWS - BAND :], "lat", [(i, i + 1) for i in range(count - 1)])
    high = lax.ppermute(planes[:, :BAND], "lat", [(i + 1, i) for i in range(count - 1)])
    far, near = pl.pallas_call(
        pack_kernel,
        out_shape=(shape(SPAN, LANES), shape(SPAN, LANES)),
        in_specs=[VMEM] * 3,
        out_specs=(VMEM, VMEM),
        cost_estimate=cost(1000000, 400000),
        compiler_params=PARAMS,
    )(planes, low, high)
    far_in = lax.ppermute(far, "grp", [(0, 3), (3, 0), (1, 2), (2, 1)])
    near_in = lax.ppermute(near, "grp", [(0, 1), (1, 0), (2, 3), (3, 2)])

    pre, heat = pl.pallas_call(
        chem_kernel,
        out_shape=(shape(SPECIES, 128, 128), shape(4, PEERS, LANES)),
        in_specs=[SMEM, SMEM, SMEM, SMEM, VMEM],
        out_specs=(VMEM, VMEM),
        scratch_shapes=[pltpu.VMEM((128, 128), jnp.float32), pltpu.VMEM((128, 128), jnp.float32)],
        cost_estimate=cost(10000000, 2000000),
        compiler_params=PARAMS,
    )(rates, pairs, heat_map, heat_coef, q)

    extended = pltpu.VMEM((PLANES, 64, LANES), jnp.float32)
    stepped, send = pl.pallas_call(
        rk_kernel,
        out_shape=(shape(PLANES, ROWS, LANES), shape(PEERS * SLOTS, LANES)),
        in_specs=[SMEM] + [VMEM] * 6,
        out_specs=(VMEM, VMEM),
        scratch_shapes=[extended] * 6 + [pltpu.VMEM((3, 128, 128), jnp.float32)],
        cost_estimate=cost(20000000, 1500000),
        compiler_params=PARAMS,
    )(coupling, planes, low, high, far_in, near_in, heat)

    received = lax.all_to_all(
        send.reshape(PEERS, SLOTS, LANES), "lon", split_axis=0, concat_axis=0, tiled=True
    )
    temperature = pl.BlockSpec((1, 128, 128), lambda i: (3, 0, 0))
    whole = pl.BlockSpec((SPECIES, 128, 128), lambda i: (0, 0, 0))
    state_out, q_out = pl.pallas_call(
        final_kernel,
        grid=(1,),
        out_shape=(shape(FIELDS, 128, 128), shape(SPECIES, 128, 128)),
        in_specs=[pl.BlockSpec((PEERS * SLOTS, LANES), lambda i: (0, 0)), temperature, whole, whole],
        out_specs=(temperature, whole),
        scratch_shapes=[pltpu.VMEM((128, 128), jnp.float32), pltpu.VMEM((3, 128, 128), jnp.float32)],
        input_output_aliases={1: 0},
        cost_estimate=cost(10000000, 2500000),
        compiler_params=PARAMS,
    )(received.reshape(PEERS * SLOTS, LANES), stepped.reshape(FIELDS, 128, 128), q, pre)
    return state_out.reshape(state.shape), q_out.reshape(tracers.shape)


def solution(mesh):
    in_specs = (
        P(None, "lon", "lat", "grp"),
        P(None, "lat", ("grp", "lon"), None),
        P(),
        P(),
        P(),
        P(),
        P(),
    )
    out_specs = (P(None, "lon", "lat", "grp"), P(None, "lat", ("grp", "lon"), None))
    return jax.shard_map(
        on_device, mesh=mesh, in_specs=in_specs, out_specs=out_specs, check_vma=False
    )
```

```python
import functools

import jax
import jax.numpy as jnp
from jax import lax
from jax.experimental import pallas as pl
from jax.experimental.pallas import tpu as pltpu
from jax.sharding import PartitionSpec as P

FIELDS = 5
LEVELS = 4
PLANES = FIELDS * LEVELS
ROWS = 32
LANES = 128
HALO = 6
BAND = 8
SPAN = ROWS + 2 * BAND
PEERS = 32
SLOTS = 16
SPECIES = 12
REACTIONS = 24


def lane_index(rows):
    return lax.broadcasted_iota(jnp.int32, (rows, LANES), 1)


def packed(source):
    lanes = lane_index(source.shape[1])
    left = source[0]
    right = pltpu.roll(source[0], HALO, 1)
    for plane in range(1, PLANES):
        keep = lanes >= HALO * plane
        left = jnp.where(keep, pltpu.roll(source[plane], HALO * plane, 1), left)
        right = jnp.where(keep, pltpu.roll(source[plane], HALO * plane + HALO, 1), right)
    odd = lax.rem(lax.axis_index("grp"), 2) == 1
    return jnp.where(odd, right, left), jnp.where(odd, left, right)


def edge_kernel(state_ref, top_ref, bottom_ref, far_ref, near_ref):
    top_ref[...] = state_ref[:, :BAND]
    bottom_ref[...] = state_ref[:, ROWS - BAND :]
    far_ref[...], near_ref[...] = packed(state_ref)


def pack_kernel(low_ref, high_ref, own_far_ref, own_near_ref, far_ref, near_ref):
    far_ref[BAND : BAND + ROWS] = own_far_ref[...]
    near_ref[BAND : BAND + ROWS] = own_near_ref[...]
    far_ref[:BAND], near_ref[:BAND] = packed(low_ref)
    far_ref[BAND + ROWS :], near_ref[BAND + ROWS :] = packed(high_ref)


def regroup(chunks):
    lanes = lane_index(ROWS)
    width = LANES // 4
    out = []
    for j in range(4):
        total = None
        for i in range(4):
            turn = (width * (i - j)) % LANES
            moved = pltpu.roll(chunks[i], turn, 1) if turn else chunks[i]
            total = moved if total is None else jnp.where(lanes >= width * i, moved, total)
        out.append(total)
    return out


def runs_here(early):
    first = lax.axis_index("grp") < lax.axis_size("grp") // 2
    return first if early else jnp.logical_not(first)


def chem_kernel(early, rates_ref, pairs_ref, map_ref, coef_ref, q_ref, *refs):
    pre_ref, heat_ref, heat_sc, turn_sc = refs[-4:]

    @pl.when(runs_here(early))
    def _():
        chemistry(rates_ref, pairs_ref, map_ref, coef_ref, q_ref, pre_ref, heat_ref, heat_sc, turn_sc)

    if not early:

        @pl.when(runs_here(True))
        def _():
            pre_ref[...] = refs[0][...]
            heat_ref[...] = refs[1][...]


def chemistry(rates_ref, pairs_ref, map_ref, coef_ref, q_ref, pre_ref, heat_ref, heat_sc, turn_sc):
    pre_ref[...] = q_ref[...]
    heat_sc[...] = jnp.zeros_like(heat_sc)

    def weight(species):
        return coef_ref[map_ref[species]]

    def react(r, carry):
        a, b, p = pairs_ref[0, r], pairs_ref[1, r], pairs_ref[2, r]
        rate = rates_ref[r] * q_ref[a] * q_ref[b]
        heat_sc[...] += (weight(p) - weight(a) - weight(b)) * rate
        pre_ref[p] += rate
        pre_ref[a] -= rate
        pre_ref[b] -= rate
        return carry

    lax.fori_loop(0, REACTIONS, react, 0)
    ordered = jnp.concatenate([heat_sc[pl.ds(y, ROWS, stride=4), :] for y in range(4)], 0)
    turn_sc[...] = jnp.transpose(ordered)
    chunks = [turn_sc[pl.ds(level, PEERS, stride=4), :] for level in range(4)]
    for y, block in enumerate(regroup(chunks)):
        heat_ref[y] = block


def lat_ends():
    lat = lax.axis_index("lat")
    return lat > 0, lat < lax.axis_size("lat") - 1


def rk_kernel(early, coupling_ref, state_ref, low_ref, high_ref, *refs):
    out_ref = refs[-7]

    @pl.when(runs_here(early))
    def _():
        whole_step(coupling_ref, state_ref, low_ref, high_ref, *refs[-7:])

    if not early:

        @pl.when(runs_here(True))
        def _():
            out_ref[...] = refs[0][...]


def whole_step(coupling_ref, state_ref, low_ref, high_ref, out_ref, sa, sb, ta, tb, ua, ub):
    has_low, has_high = lat_ends()
    base = 16

    sb[...] = jnp.zeros_like(sb)
    for plane in range(PLANES):
        sa[plane, base - BAND : base, :] = low_ref[plane]
        sa[plane, base : base + ROWS, :] = state_ref[plane]
        sa[plane, base + ROWS : base + ROWS + BAND, :] = high_ref[plane]

    lane8 = lane_index(8)
    weights = [
        [coupling_ref[f, g] + (0.6 if f == g else 0.0) for g in range(FIELDS)] for f in range(FIELDS)
    ]

    def apply(a_ref, b_ref, z, row, both):
        centers_a = [a_ref[f * LEVELS + z, row : row + 8, :] for f in range(FIELDS)]
        centers_b = [b_ref[f * LEVELS + z, row : row + 8, :] for f in range(FIELDS)]

        def along_lanes(f):
            moved = {}
            for j in (1, 2, -1, -2):
                ra = pltpu.roll(centers_a[f], -j % LANES, 1)
                rb = pltpu.roll(centers_b[f], -j % LANES, 1)
                inner = lane8 < LANES - j if j > 0 else lane8 >= -j
                moved[j] = (jnp.where(inner, ra, rb), jnp.where(inner, rb, ra) if both else None)
            return moved

        result = []
        for f in range(FIELDS):
            moved = along_lanes(f)
            pieces = []
            for part, ref, centers in ((0, a_ref, centers_a), (1, b_ref, centers_b)):
                if part == 1 and not both:
                    break
                x = {j: ref[f * LEVELS + z, row + j : row + j + 8, :] for j in (1, 2, -1, -2)}
                total = -0.1 * (x[1] + moved[1][part]) + 0.3 * (x[-1] + moved[-1][part])
                total = total + 0.025 * ((x[2] - x[-2]) + (moved[2][part] - moved[-2][part]))
                for g in range(FIELDS):
                    total = total + weights[f][g] * centers[g]
                pieces.append(total)
            result.append(pieces)
        return result

    first, last = base - BAND, base + ROWS

    def masked(value, row):
        if row == first:
            return jnp.where(has_low, value, 0.0)
        if row == last:
            return jnp.where(has_high, value, 0.0)
        return value

    def stage_one(z, carry):
        for row in range(first, last + 8, 8):
            for f, (a, b) in enumerate(apply(sa, sb, z, row, True)):
                ta[f * LEVELS + z, row : row + 8, :] = masked(a, row)
                tb[f * LEVELS + z, row : row + 8, :] = masked(b, row)
        return carry

    def stage_two(z, carry):
        for row in range(first, last + 8, 8):
            for f, (a, b) in enumerate(apply(ta, tb, z, row, True)):
                plane = f * LEVELS + z
                ua[plane, row : row + 8, :] = masked(0.75 * sa[plane, row : row + 8, :] + 0.25 * a, row)
                ub[plane, row : row + 8, :] = masked(0.75 * sb[plane, row : row + 8, :] + 0.25 * b, row)
        return carry

    def stage_three(z, carry):
        for row in range(base, last, 8):
            for f, (a,) in enumerate(apply(ua, ub, z, row, False)):
                plane = f * LEVELS + z
                value = sa[plane, row : row + 8, :] * (1.0 / 3.0) + (2.0 / 3.0) * a
                out_ref[plane, row - base : row - base + 8, :] = value
        return carry

    lax.fori_loop(0, LEVELS, stage_one, 0)
    lax.fori_loop(0, LEVELS, stage_two, 0)
    lax.fori_loop(0, LEVELS, stage_three, 0)


def edge_step_kernel(
    coupling_ref, main_ref, far_ref, near_ref, heat_ref, out_ref, send_ref, sa, sb, ta, tb, ua, ub, turn_sc
):
    odd = lax.rem(lax.axis_index("grp"), 2) == 1
    has_low, has_high = lat_ends()
    pad = 8
    zero = jnp.zeros((SPAN, LANES), jnp.float32)
    sa[pad : pad + SPAN, :] = jnp.where(odd, near_ref[...], far_ref[...])
    sa[pad + SPAN : pad + 2 * SPAN, :] = zero
    sb[pad : pad + SPAN, :] = zero
    sb[pad + SPAN : pad + 2 * SPAN, :] = jnp.where(odd, far_ref[...], near_ref[...])

    lanes = lane_index(8)
    column = lax.rem(lanes, HALO)
    field = lanes // (HALO * LEVELS)
    mixes = {}
    for d in range(1 - FIELDS, FIELDS):
        total = jnp.zeros((8, LANES), jnp.float32)
        for f in range(max(d, 0), min(FIELDS, FIELDS + d)):
            total = jnp.where(field == f, coupling_ref[f, f - d] + (0.6 if d == 0 else 0.0), total)
        mixes[d] = total

    def turn(value, by):
        return pltpu.roll(value, by % LANES, 1) if by % LANES else value

    def apply(a_ref, b_ref, row):
        a, b = a_ref[row : row + 8, :], b_ref[row : row + 8, :]
        ya, yb = {}, {}
        for j in (1, 2):
            inside, behind = column < HALO - j, column >= j
            ya[j] = jnp.where(inside, turn(a, -j), turn(b, HALO - j))
            yb[j] = jnp.where(inside, turn(b, -j), 0.0)
            ya[-j] = jnp.where(behind, turn(a, j), 0.0)
            yb[-j] = jnp.where(behind, turn(b, j), turn(a, j - HALO))
        out = []
        for value, ref, y in ((a, a_ref, ya), (b, b_ref, yb)):
            x = {j: ref[row + j : row + j + 8, :] for j in (1, 2, -1, -2)}
            total = -0.1 * (x[1] + y[1]) + 0.3 * (x[-1] + y[-1])
            total = total + 0.025 * ((x[2] - x[-2]) + (y[2] - y[-2]))
            for d, mix in mixes.items():
                total = total + mix * turn(value, HALO * LEVELS * d)
            out.append(total)
        return out

    def masked(value, row):
        place = (row - pad) % SPAN
        if place < BAND:
            return jnp.where(has_low, value, 0.0)
        if place >= BAND + ROWS:
            return jnp.where(has_high, value, 0.0)
        return value

    every = range(pad, pad + 2 * SPAN, 8)
    for row in every:
        a, b = apply(sa, sb, row)
        ta[row : row + 8, :] = masked(a, row)
        tb[row : row + 8, :] = masked(b, row)
    for row in every:
        a, b = apply(ta, tb, row)
        ua[row : row + 8, :] = masked(0.75 * sa[row : row + 8, :] + 0.25 * a, row)
        ub[row : row + 8, :] = masked(0.75 * sb[row : row + 8, :] + 0.25 * b, row)
    for row in range(pad + BAND, pad + BAND + ROWS, 8):
        _, b = apply(ua, ub, row)
        a, _ = apply(ua, ub, row + SPAN)
        first, final = (2.0 / 3.0) * b, (2.0 / 3.0) * a
        place = row - pad - BAND
        for plane in range(PLANES):
            gain = jnp.where(lanes < HALO, turn(first, -HALO * plane), 0.0)
            gain = jnp.where(lanes >= LANES - HALO, turn(final, LANES - HALO - HALO * plane), gain)
            out_ref[plane, place : place + 8, :] = main_ref[plane, place : place + 8, :] + gain

    for f in range(3):
        plane = jnp.concatenate([out_ref[f * LEVELS + z] for z in range(LEVELS)], 0)
        turn_sc[f] = jnp.transpose(plane)
        chunks = [turn_sc[f, pl.ds(y, PEERS, stride=4), :] for y in range(4)]
        for level, block in enumerate(regroup(chunks)):
            send_ref[pl.ds(4 * f + level, PEERS, stride=SLOTS), :] = block
    for y in range(4):
        send_ref[pl.ds(12 + y, PEERS, stride=SLOTS), :] = heat_ref[y]


def final_kernel(recv_ref, temp_ref, q_ref, pre_ref, temp_out_ref, q_out_ref, turn_sc, wind_sc):
    for y in range(4):
        turn_sc[pl.ds(y, PEERS, stride=4), :] = recv_ref[pl.ds(12 + y, PEERS, stride=SLOTS), :]
    temp_out_ref[0] = temp_ref[0] + 0.5 * jnp.transpose(turn_sc[...])
    for f in range(3):
        for level in range(4):
            turn_sc[pl.ds(level, PEERS, stride=4), :] = recv_ref[pl.ds(4 * f + level, PEERS, stride=SLOTS), :]
        columns = jnp.transpose(turn_sc[...])
        for y in range(4):
            wind_sc[f, pl.ds(y, ROWS, stride=4), :] = columns[y * ROWS : (y + 1) * ROWS]

    chunk = 32
    lanes = lane_index(chunk)

    def clamped(value):
        higher = jnp.where(lanes == LANES - 1, value, pltpu.roll(value, LANES - 1, 1))
        lower = jnp.where(lanes == 0, value, pltpu.roll(value, 1, 1))
        return higher, lower

    for start in range(0, 128, chunk):
        rows = slice(start, start + chunk)
        shear = None
        for f in range(2):
            higher, lower = clamped(wind_sc[f, rows, :])
            square = (higher - lower) * (higher - lower)
            shear = square if shear is None else shear + square
        mixing = 0.2 * shear / (1.0 + shear)
        vertical = wind_sc[2, rows, :]
        speed = 0.4 * vertical / (1.0 + jnp.abs(vertical))
        up = mixing - jnp.minimum(speed, 0.0)
        down = mixing + jnp.maximum(speed, 0.0)
        for s in range(SPECIES):
            value = q_ref[s, rows, :]
            higher, lower = clamped(value)
            q_out_ref[s, rows, :] = pre_ref[s, rows, :] + (up * (higher - value) - down * (value - lower))


VMEM = pl.BlockSpec(memory_space=pltpu.VMEM)
SMEM = pl.BlockSpec(memory_space=pltpu.SMEM)
PARAMS = pltpu.CompilerParams(vmem_limit_bytes=16 * 1024 * 1024)


def shape(*dims):
    return jax.ShapeDtypeStruct(dims, jnp.float32)


def cost(flops, data):
    return pl.CostEstimate(flops=flops, bytes_accessed=data, transcendentals=0)


def on_device(state, tracers, coupling, rates, pairs, heat_map, heat_coef):
    planes = state.reshape(PLANES, ROWS, LANES)
    q = tracers.reshape(SPECIES, 128, 128)

    top, bottom, own_far, own_near = pl.pallas_call(
        edge_kernel,
        out_shape=(shape(PLANES, BAND, LANES),) * 2 + (shape(ROWS, LANES),) * 2,
        in_specs=[VMEM],
        out_specs=(VMEM,) * 4,
        cost_estimate=cost(1000000, 500000),
        compiler_params=PARAMS,
    )(planes)
    count = lax.axis_size("lat")
    low = lax.ppermute(bottom, "lat", [(i, i + 1) for i in range(count - 1)])
    high = lax.ppermute(top, "lat", [(i + 1, i) for i in range(count - 1)])
    reactants = (rates, pairs.T, heat_map, heat_coef, q)

    def chem(early, *before):
        return pl.pallas_call(
            functools.partial(chem_kernel, early),
            out_shape=(shape(SPECIES, 128, 128), shape(4, PEERS, LANES)),
            in_specs=[SMEM, SMEM, SMEM, SMEM, VMEM] + [VMEM] * len(before),
            out_specs=(VMEM, VMEM),
            scratch_shapes=[pltpu.VMEM((128, 128), jnp.float32), pltpu.VMEM((128, 128), jnp.float32)],
            input_output_aliases={5 + i: i for i in range(len(before))},
            cost_estimate=cost(10000000, 2000000),
            compiler_params=PARAMS,
        )(*reactants, *before)

    extended = pltpu.VMEM((PLANES, 64, LANES), jnp.float32)

    def rk(early, *before):
        return pl.pallas_call(
            functools.partial(rk_kernel, early),
            out_shape=shape(PLANES, ROWS, LANES),
            in_specs=[SMEM] + [VMEM] * (3 + len(before)),
            out_specs=VMEM,
            scratch_shapes=[extended] * 6,
            input_output_aliases={4 + i: i for i in range(len(before))},
            cost_estimate=cost(20000000, 1500000),
            compiler_params=PARAMS,
        )(coupling, planes, low, high, *before)

    pre, heat = chem(True)
    low, high, heat = lax.optimization_barrier((low, high, heat))
    main = rk(True)
    low, high, main = lax.optimization_barrier((low, high, main))
    far, near = pl.pallas_call(
        pack_kernel,
        out_shape=(shape(SPAN, LANES), shape(SPAN, LANES)),
        in_specs=[VMEM] * 4,
        out_specs=(VMEM, VMEM),
        cost_estimate=cost(1000000, 400000),
        compiler_params=PARAMS,
    )(low, high, own_far, own_near)
    far, near, low, high, main, pre, heat = lax.optimization_barrier((far, near, low, high, main, pre, heat))
    far_in = lax.ppermute(far, "grp", [(0, 3), (3, 0), (1, 2), (2, 1)])
    near_in = lax.ppermute(near, "grp", [(0, 1), (1, 0), (2, 3), (3, 2)])
    pre, heat = chem(False, pre, heat)
    main = rk(False, main)
    window = pltpu.VMEM((2 * SPAN + 16, LANES), jnp.float32)
    stepped, send = pl.pallas_call(
        edge_step_kernel,
        out_shape=(shape(PLANES, ROWS, LANES), shape(PEERS * SLOTS, LANES)),
        in_specs=[SMEM] + [VMEM] * 4,
        out_specs=(VMEM, VMEM),
        scratch_shapes=[window] * 6 + [pltpu.VMEM((3, 128, 128), jnp.float32)],
        cost_estimate=cost(2000000, 1000000),
        compiler_params=PARAMS,
    )(coupling, main, far_in, near_in, heat)

    received = lax.all_to_all(
        send.reshape(PEERS, SLOTS, LANES), "lon", split_axis=0, concat_axis=0, tiled=True
    )
    temperature = pl.BlockSpec((1, 128, 128), lambda i: (3, 0, 0))
    whole = pl.BlockSpec((SPECIES, 128, 128), lambda i: (0, 0, 0))
    state_out, q_out = pl.pallas_call(
        final_kernel,
        grid=(1,),
        out_shape=(shape(FIELDS, 128, 128), shape(SPECIES, 128, 128)),
        in_specs=[pl.BlockSpec((PEERS * SLOTS, LANES), lambda i: (0, 0)), temperature, whole, whole],
        out_specs=(temperature, whole),
        scratch_shapes=[pltpu.VMEM((128, 128), jnp.float32), pltpu.VMEM((3, 128, 128), jnp.float32)],
        input_output_aliases={1: 0},
        cost_estimate=cost(10000000, 2500000),
        compiler_params=PARAMS,
    )(received.reshape(PEERS * SLOTS, LANES), stepped.reshape(FIELDS, 128, 128), q, pre)
    return state_out.reshape(state.shape), q_out.reshape(tracers.shape)


def solution(mesh):
    in_specs = (
        P(None, "lon", "lat", "grp"),
        P(None, "lat", ("grp", "lon"), None),
        P(),
        P(),
        P(),
        P(),
        P(),
    )
    out_specs = (P(None, "lon", "lat", "grp"), P(None, "lat", ("grp", "lon"), None))
    return jax.shard_map(
        on_device, mesh=mesh, in_specs=in_specs, out_specs=out_specs, check_vma=False
    )
```

```python
import functools

import jax
import jax.numpy as jnp
from jax import lax
from jax.experimental import pallas as pl
from jax.experimental.pallas import tpu as pltpu
from jax.sharding import PartitionSpec as P

FIELDS = 5
LEVELS = 4
PLANES = FIELDS * LEVELS
ROWS = 32
LANES = 128
HALO = 6
BAND = 8
SPAN = ROWS + 2 * BAND
PEERS = 32
SLOTS = 16
SPECIES = 12
REACTIONS = 24


def lane_index(rows):
    return lax.broadcasted_iota(jnp.int32, (rows, LANES), 1)


def packed(source):
    lanes = lane_index(source.shape[1])
    left = source[0]
    right = pltpu.roll(source[0], HALO, 1)
    for plane in range(1, PLANES):
        keep = lanes >= HALO * plane
        left = jnp.where(keep, pltpu.roll(source[plane], HALO * plane, 1), left)
        right = jnp.where(keep, pltpu.roll(source[plane], HALO * plane + HALO, 1), right)
    odd = lax.rem(lax.axis_index("grp"), 2) == 1
    return jnp.where(odd, right, left), jnp.where(odd, left, right)


def own_kernel(state_ref, *refs):
    far_ref, near_ref = refs[-2:]
    far_ref[...], near_ref[...] = packed(state_ref)


def pack_kernel(low_ref, high_ref, own_far_ref, own_near_ref, far_ref, near_ref):
    far_ref[BAND : BAND + ROWS] = own_far_ref[...]
    near_ref[BAND : BAND + ROWS] = own_near_ref[...]
    far_ref[:BAND], near_ref[:BAND] = packed(low_ref)
    far_ref[BAND + ROWS :], near_ref[BAND + ROWS :] = packed(high_ref)


def regroup(chunks):
    lanes = lane_index(ROWS)
    chunks = list(chunks)
    for bit in (2, 1):
        width = bit * LANES // 4
        lower = lax.rem(lanes // width, 2) == 0
        for i in range(4):
            if not i & bit:
                a, b = chunks[i], chunks[i + bit]
                chunks[i] = jnp.where(lower, a, pltpu.roll(b, width, 1))
                chunks[i + bit] = jnp.where(lower, pltpu.roll(a, LANES - width, 1), b)
    return chunks


def runs_here(early):
    first = lax.axis_index("grp") < lax.axis_size("grp") // 2
    return first if early else jnp.logical_not(first)


def local_kernel(early, *refs):
    inputs, outputs, scratch = refs[:9], refs[-13:-9], refs[-9:]
    rates_ref, pairs_ref, map_ref, coef_ref, q_ref, coupling_ref, state_ref, low_ref, high_ref = inputs
    pre_ref, heat_ref, main_ref, send_ref = outputs

    @pl.when(runs_here(early))
    def _():
        whole_step(coupling_ref, state_ref, low_ref, high_ref, main_ref, send_ref, *scratch[:6], scratch[8])
        chemistry(rates_ref, pairs_ref, map_ref, coef_ref, q_ref, pre_ref, heat_ref, *scratch[6:8])
        for y in range(4):
            send_ref[pl.ds(12 + y, PEERS, stride=SLOTS), :] = heat_ref[y]


def chemistry(rates_ref, pairs_ref, map_ref, coef_ref, q_ref, pre_ref, heat_ref, heat_sc, turn_sc):
    pre_ref[...] = q_ref[...]
    heat_sc[...] = jnp.zeros_like(heat_sc)

    def weight(species):
        return coef_ref[map_ref[species]]

    def react(r, carry):
        a, b, p = pairs_ref[0, r], pairs_ref[1, r], pairs_ref[2, r]
        rate = rates_ref[r] * q_ref[a] * q_ref[b]
        heat_sc[...] += (weight(p) - weight(a) - weight(b)) * rate
        pre_ref[p] += rate
        pre_ref[a] -= rate
        pre_ref[b] -= rate
        return carry

    lax.fori_loop(0, REACTIONS, react, 0)
    ordered = jnp.concatenate([heat_sc[pl.ds(y, ROWS, stride=4), :] for y in range(4)], 0)
    turn_sc[...] = jnp.transpose(ordered)
    chunks = [turn_sc[pl.ds(level, PEERS, stride=4), :] for level in range(4)]
    for y, block in enumerate(regroup(chunks)):
        heat_ref[y] = block


def lat_ends():
    lat = lax.axis_index("lat")
    return lat > 0, lat < lax.axis_size("lat") - 1


def whole_step(coupling_ref, state_ref, low_ref, high_ref, out_ref, send_ref, sa, sb, ta, tb, ua, ub, turn_sc):
    has_low, has_high = lat_ends()
    base = 16

    sb[...] = jnp.zeros_like(sb)
    for plane in range(PLANES):
        sa[plane, base - BAND : base, :] = low_ref[plane]
        sa[plane, base : base + ROWS, :] = state_ref[plane]
        sa[plane, base + ROWS : base + ROWS + BAND, :] = high_ref[plane]

    lane8 = lane_index(8)
    weights = [
        [coupling_ref[f, g] + (0.6 if f == g else 0.0) for g in range(FIELDS)] for f in range(FIELDS)
    ]

    def apply(a_ref, b_ref, z, row, both):
        centers_a = [a_ref[f * LEVELS + z, row : row + 8, :] for f in range(FIELDS)]
        centers_b = [b_ref[f * LEVELS + z, row : row + 8, :] for f in range(FIELDS)]

        def along_lanes(f):
            moved = {}
            for j in (1, 2, -1, -2):
                ra = pltpu.roll(centers_a[f], -j % LANES, 1)
                rb = pltpu.roll(centers_b[f], -j % LANES, 1)
                inner = lane8 < LANES - j if j > 0 else lane8 >= -j
                moved[j] = (jnp.where(inner, ra, rb), jnp.where(inner, rb, ra) if both else None)
            return moved

        result = []
        for f in range(FIELDS):
            moved = along_lanes(f)
            pieces = []
            for part, ref, centers in ((0, a_ref, centers_a), (1, b_ref, centers_b)):
                if part == 1 and not both:
                    break
                x = {j: ref[f * LEVELS + z, row + j : row + j + 8, :] for j in (1, 2, -1, -2)}
                total = -0.1 * (x[1] + moved[1][part]) + 0.3 * (x[-1] + moved[-1][part])
                total = total + 0.025 * ((x[2] - x[-2]) + (moved[2][part] - moved[-2][part]))
                for g in range(FIELDS):
                    total = total + weights[f][g] * centers[g]
                pieces.append(total)
            result.append(pieces)
        return result

    first, last = base - BAND, base + ROWS

    def masked(value, row):
        if row == first:
            return jnp.where(has_low, value, 0.0)
        if row == last:
            return jnp.where(has_high, value, 0.0)
        return value

    def stage_one(z, carry):
        for row in range(first, last + 8, 8):
            for f, (a, b) in enumerate(apply(sa, sb, z, row, True)):
                ta[f * LEVELS + z, row : row + 8, :] = masked(a, row)
                tb[f * LEVELS + z, row : row + 8, :] = masked(b, row)
        return carry

    def stage_two(z, carry):
        for row in range(first, last + 8, 8):
            for f, (a, b) in enumerate(apply(ta, tb, z, row, True)):
                plane = f * LEVELS + z
                ua[plane, row : row + 8, :] = masked(0.75 * sa[plane, row : row + 8, :] + 0.25 * a, row)
                ub[plane, row : row + 8, :] = masked(0.75 * sb[plane, row : row + 8, :] + 0.25 * b, row)
        return carry

    def stage_three(z, carry):
        for row in range(base, last, 8):
            for f, (a,) in enumerate(apply(ua, ub, z, row, False)):
                plane = f * LEVELS + z
                value = sa[plane, row : row + 8, :] * (1.0 / 3.0) + (2.0 / 3.0) * a
                out_ref[plane, row - base : row - base + 8, :] = value
        return carry

    lax.fori_loop(0, LEVELS, stage_one, 0)
    lax.fori_loop(0, LEVELS, stage_two, 0)
    lax.fori_loop(0, LEVELS, stage_three, 0)

    for f in range(3):
        plane = jnp.concatenate([out_ref[f * LEVELS + z] for z in range(LEVELS)], 0)
        turn_sc[f] = jnp.transpose(plane)
        chunks = [turn_sc[f, pl.ds(y, PEERS, stride=4), :] for y in range(4)]
        for level, block in enumerate(regroup(chunks)):
            send_ref[pl.ds(4 * f + level, PEERS, stride=SLOTS), :] = block


def edge_step_kernel(
    once_ref, twice_ref, main_ref, sent_ref, far_ref, near_ref, out_ref, send_ref, sa, sb, ta, tb, ua, ub, turn_sc
):
    odd = lax.rem(lax.axis_index("grp"), 2) == 1
    has_low, has_high = lat_ends()
    pad = 8
    zero = jnp.zeros((SPAN, LANES), jnp.float32)
    sa[pad : pad + SPAN, :] = jnp.where(odd, near_ref[...], far_ref[...])
    sa[pad + SPAN : pad + 2 * SPAN, :] = zero
    sb[pad : pad + SPAN, :] = zero
    sb[pad + SPAN : pad + 2 * SPAN, :] = jnp.where(odd, far_ref[...], near_ref[...])

    lanes = lane_index(8)
    column = lax.rem(lanes, HALO)
    field = lanes // (HALO * LEVELS)

    def mix_of(ref):
        mixes = {}
        for d in range(1 - FIELDS, FIELDS):
            total = jnp.zeros((8, LANES), jnp.float32)
            for f in range(max(d, 0), min(FIELDS, FIELDS + d)):
                total = jnp.where(field == f, ref[f, f - d], total)
            mixes[d] = total
        return mixes

    once, twice = mix_of(once_ref), mix_of(twice_ref)

    def turn(value, by):
        return pltpu.roll(value, by % LANES, 1) if by % LANES else value

    def apply(a_ref, b_ref, row, parts="ab"):
        a, b = a_ref[row : row + 8, :], b_ref[row : row + 8, :]
        out = []
        for part in parts:
            y = {}
            for j in (1, 2):
                inside, behind = column < HALO - j, column >= j
                if part == "a":
                    y[j] = jnp.where(inside, turn(a, -j), turn(b, HALO - j))
                    y[-j] = jnp.where(behind, turn(a, j), 0.0)
                else:
                    y[j] = jnp.where(inside, turn(b, -j), 0.0)
                    y[-j] = jnp.where(behind, turn(b, j), turn(a, j - HALO))
            ref = a_ref if part == "a" else b_ref
            x = {j: ref[row + j : row + j + 8, :] for j in (1, 2, -1, -2)}
            total = -0.1 * (x[1] + y[1]) + 0.3 * (x[-1] + y[-1])
            total = total + 0.025 * ((x[2] - x[-2]) + (y[2] - y[-2]))
            out.append(total - 0.4 * (a if part == "a" else b))
        return out

    def mixed(mixes, value):
        total = None
        for d, mix in mixes.items():
            term = mix * turn(value, HALO * LEVELS * d)
            total = term if total is None else total + term
        return total

    def masked(value, row):
        place = (row - pad) % SPAN
        if place < BAND:
            return jnp.where(has_low, value, 0.0)
        if place >= BAND + ROWS:
            return jnp.where(has_high, value, 0.0)
        return value

    every = range(pad, pad + 2 * SPAN, 8)
    for row in every:
        a, b = apply(sa, sb, row)
        ta[row : row + 8, :] = masked(a, row)
        tb[row : row + 8, :] = masked(b, row)
    for row in every:
        a, b = apply(ta, tb, row)
        ua[row : row + 8, :] = masked(a, row)
        ub[row : row + 8, :] = masked(b, row)
    firsts, finals = [], []
    for row in range(pad + BAND, pad + BAND + ROWS, 8):
        (b,) = apply(ua, ub, row, "b")
        (a,) = apply(ua, ub, row + SPAN, "a")
        first = mixed(twice, tb[row : row + 8, :]) + mixed(once, 0.5 * ub[row : row + 8, :]) + b * (1.0 / 6.0)
        other = row + SPAN
        final = mixed(twice, ta[other : other + 8, :]) + mixed(once, 0.5 * ua[other : other + 8, :]) + a * (1.0 / 6.0)
        firsts.append(first)
        finals.append(final)
        place = row - pad - BAND
        for plane in range(PLANES):
            gain = jnp.where(lanes < HALO, turn(first, -HALO * plane), 0.0)
            gain = jnp.where(lanes >= LANES - HALO, turn(final, LANES - HALO - HALO * plane), gain)
            out_ref[plane, place : place + 8, :] = main_ref[plane, place : place + 8, :] + gain

    send_ref[...] = sent_ref[...]
    winds = 3 * LEVELS
    lanes12 = lane_index(winds)
    zeros = jnp.zeros((LANES - ROWS, LANES), jnp.float32)
    for side, values in ((0, firsts), (1, finals)):
        turn_sc[side] = jnp.transpose(jnp.concatenate(values + [zeros], 0))
        for peer in (0, 1) if side == 0 else (PEERS - 2, PEERS - 1):
            gain = jnp.zeros((winds, LANES), jnp.float32)
            for y in range(4):
                c = 4 * peer + y - (LANES - HALO if side else 0)
                if 0 <= c < HALO:
                    part = turn_sc[side, pl.ds(c, winds, stride=HALO), :]
                    here = jnp.logical_and(lanes12 >= ROWS * y, lanes12 < ROWS * y + ROWS)
                    gain = jnp.where(here, turn(part, ROWS * y), gain)
            send_ref[peer * SLOTS : peer * SLOTS + winds, :] += gain


def final_kernel(recv_ref, stepped_ref, q_ref, pre_ref, state_out_ref, q_out_ref, turn_sc, wind_sc, temp_sc, q_sc, sems):
    copies = []

    def send_out(source, target):
        copy = pltpu.make_async_copy(source, target, sems.at[len(copies)])
        copy.start()
        copies.append(copy)

    send_out(stepped_ref.at[0:3], state_out_ref.at[0:3])
    send_out(stepped_ref.at[4:5], state_out_ref.at[4:5])
    for f in range(3):
        for level in range(4):
            turn_sc[pl.ds(level, PEERS, stride=4), :] = recv_ref[pl.ds(4 * f + level, PEERS, stride=SLOTS), :]
        columns = jnp.transpose(turn_sc[...])
        for y in range(4):
            wind_sc[f, pl.ds(y, ROWS, stride=4), :] = columns[y * ROWS : (y + 1) * ROWS]

    chunk = 32
    lanes = lane_index(chunk)

    def clamped(value):
        higher = jnp.where(lanes == LANES - 1, value, pltpu.roll(value, LANES - 1, 1))
        lower = jnp.where(lanes == 0, value, pltpu.roll(value, 1, 1))
        return higher, lower

    for start in range(0, 128, chunk):
        rows = slice(start, start + chunk)
        shear = None
        for f in range(2):
            higher, lower = clamped(wind_sc[f, rows, :])
            square = (higher - lower) * (higher - lower)
            shear = square if shear is None else shear + square
        mixing = 0.2 * shear / (1.0 + shear)
        vertical = wind_sc[2, rows, :]
        speed = 0.4 * vertical / (1.0 + jnp.abs(vertical))
        up = mixing - jnp.minimum(speed, 0.0)
        down = mixing + jnp.maximum(speed, 0.0)
        for s in range(SPECIES):
            value = q_ref[s, rows, :]
            higher, lower = clamped(value)
            q_sc[s, rows, :] = pre_ref[s, rows, :] + (up * (higher - value) - down * (value - lower))
        send_out(q_sc.at[:, rows, :], q_out_ref.at[:, rows, :])
        if start == 0:
            for y in range(4):
                turn_sc[pl.ds(y, PEERS, stride=4), :] = recv_ref[pl.ds(12 + y, PEERS, stride=SLOTS), :]
            temp_sc[0] = stepped_ref[3] + 0.5 * jnp.transpose(turn_sc[...])
            send_out(temp_sc, state_out_ref.at[3:4])
    for copy in copies:
        copy.wait()


VMEM = pl.BlockSpec(memory_space=pltpu.VMEM)
SMEM = pl.BlockSpec(memory_space=pltpu.SMEM)
PARAMS = pltpu.CompilerParams(vmem_limit_bytes=16 * 1024 * 1024)


def shape(*dims):
    return jax.ShapeDtypeStruct(dims, jnp.float32)


def cost(flops, data):
    return pl.CostEstimate(flops=flops, bytes_accessed=data, transcendentals=0)


def on_device(state, tracers, coupling, rates, pairs, heat_map, heat_coef):
    planes = state.reshape(PLANES, ROWS, LANES)
    q = tracers.reshape(SPECIES, 128, 128)

    count = lax.axis_size("lat")
    low = lax.ppermute(planes[:, ROWS - BAND :], "lat", [(i, i + 1) for i in range(count - 1)])
    high = lax.ppermute(planes[:, :BAND], "lat", [(i + 1, i) for i in range(count - 1)])
    once = jnp.eye(FIELDS, dtype=jnp.float32) + coupling
    squared = jnp.sum(coupling[:, :, None] * coupling[None, :, :], 1)
    twice = once + 0.5 * squared
    reactants = (rates, pairs.T, heat_map, heat_coef, q)

    own_far, own_near = pl.pallas_call(
        own_kernel,
        out_shape=(shape(ROWS, LANES),) * 2,
        in_specs=[VMEM] + [SMEM] * 4 + [VMEM, SMEM],
        out_specs=(VMEM,) * 2,
        cost_estimate=cost(1000000, 400000),
        compiler_params=PARAMS,
    )(planes, *reactants, coupling)
    extended = pltpu.VMEM((PLANES, 64, LANES), jnp.float32)
    square = pltpu.VMEM((128, 128), jnp.float32)

    def local(early, *before):
        return pl.pallas_call(
            functools.partial(local_kernel, early),
            out_shape=(
                shape(SPECIES, 128, 128),
                shape(4, PEERS, LANES),
                shape(PLANES, ROWS, LANES),
                shape(PEERS * SLOTS, LANES),
            ),
            in_specs=[SMEM] * 4 + [VMEM, SMEM] + [VMEM] * (3 + len(before)),
            out_specs=(VMEM,) * 4,
            scratch_shapes=[extended] * 6 + [square] * 2 + [pltpu.VMEM((3, 128, 128), jnp.float32)],
            input_output_aliases={9 + i: i for i in range(len(before))},
            cost_estimate=cost(30000000, 3000000),
            compiler_params=PARAMS,
        )(*reactants, coupling, planes, low, high, *before)

    done = local(True)
    low, high, once, twice, *done = lax.optimization_barrier((low, high, once, twice, *done))
    far, near = pl.pallas_call(
        pack_kernel,
        out_shape=(shape(SPAN, LANES), shape(SPAN, LANES)),
        in_specs=[VMEM] * 4,
        out_specs=(VMEM, VMEM),
        cost_estimate=cost(1000000, 400000),
        compiler_params=PARAMS,
    )(low, high, own_far, own_near)
    far, near, low, high, *done = lax.optimization_barrier((far, near, low, high, *done))
    far_in = lax.ppermute(far, "grp", [(0, 3), (3, 0), (1, 2), (2, 1)])
    near_in = lax.ppermute(near, "grp", [(0, 1), (1, 0), (2, 3), (3, 2)])
    pre, _, main, sent = local(False, *done)
    window = pltpu.VMEM((2 * SPAN + 16, LANES), jnp.float32)
    stepped, send = pl.pallas_call(
        edge_step_kernel,
        out_shape=(shape(PLANES, ROWS, LANES), shape(PEERS * SLOTS, LANES)),
        in_specs=[SMEM] * 2 + [VMEM] * 4,
        out_specs=(VMEM, VMEM),
        scratch_shapes=[window] * 6 + [pltpu.VMEM((2, 128, 128), jnp.float32)],
        input_output_aliases={3: 1},
        cost_estimate=cost(2000000, 1000000),
        compiler_params=PARAMS,
    )(once, twice, main, sent, far_in, near_in)

    received = lax.all_to_all(
        send.reshape(PEERS, SLOTS, LANES), "lon", split_axis=0, concat_axis=0, tiled=True
    )
    outside = pl.BlockSpec(memory_space=pltpu.HBM)
    state_out, q_out = pl.pallas_call(
        final_kernel,
        out_shape=(shape(FIELDS, 128, 128), shape(SPECIES, 128, 128)),
        in_specs=[VMEM] * 4,
        out_specs=(outside,) * 2,
        scratch_shapes=[
            square,
            pltpu.VMEM((3, 128, 128), jnp.float32),
            pltpu.VMEM((1, 128, 128), jnp.float32),
            pltpu.VMEM((SPECIES, 128, 128), jnp.float32),
            pltpu.SemaphoreType.DMA((7,)),
        ],
        cost_estimate=cost(10000000, 2500000),
        compiler_params=PARAMS,
    )(received.reshape(PEERS * SLOTS, LANES), stepped.reshape(FIELDS, 128, 128), q, pre)
    return state_out.reshape(state.shape), q_out.reshape(tracers.shape)


def solution(mesh):
    in_specs = (
        P(None, "lon", "lat", "grp"),
        P(None, "lat", ("grp", "lon"), None),
        P(),
        P(),
        P(),
        P(),
        P(),
    )
    out_specs = (P(None, "lon", "lat", "grp"), P(None, "lat", ("grp", "lon"), None))
    return jax.shard_map(
        on_device, mesh=mesh, in_specs=in_specs, out_specs=out_specs, check_vma=False
    )
```

```python
import functools

import jax
import jax.numpy as jnp
from jax import lax
from jax.experimental import pallas as pl
from jax.experimental.pallas import tpu as pltpu
from jax.sharding import PartitionSpec as P

FIELDS = 5
LEVELS = 4
PLANES = FIELDS * LEVELS
ROWS = 32
LANES = 128
HALO = 6
BAND = 8
SPAN = ROWS + 2 * BAND
PEERS = 32
SLOTS = 16
SPECIES = 12
REACTIONS = 24


def lane_index(rows):
    return lax.broadcasted_iota(jnp.int32, (rows, LANES), 1)


def packed(source):
    lanes = lane_index(source.shape[1])
    left = source[0]
    right = pltpu.roll(source[0], HALO, 1)
    for plane in range(1, PLANES):
        keep = lanes >= HALO * plane
        left = jnp.where(keep, pltpu.roll(source[plane], HALO * plane, 1), left)
        right = jnp.where(keep, pltpu.roll(source[plane], HALO * plane + HALO, 1), right)
    odd = lax.rem(lax.axis_index("grp"), 2) == 1
    return jnp.where(odd, right, left), jnp.where(odd, left, right)


def own_kernel(state_ref, far_ref, near_ref):
    far_ref[...], near_ref[...] = packed(state_ref)


def pack_kernel(low_ref, high_ref, own_far_ref, own_near_ref, far_ref, near_ref):
    far_ref[BAND : BAND + ROWS] = own_far_ref[...]
    near_ref[BAND : BAND + ROWS] = own_near_ref[...]
    far_ref[:BAND], near_ref[:BAND] = packed(low_ref)
    far_ref[BAND + ROWS :], near_ref[BAND + ROWS :] = packed(high_ref)


def regroup(chunks):
    lanes = lane_index(ROWS)
    chunks = list(chunks)
    for bit in (2, 1):
        width = bit * LANES // 4
        lower = lax.rem(lanes // width, 2) == 0
        for i in range(4):
            if not i & bit:
                a, b = chunks[i], chunks[i + bit]
                chunks[i] = jnp.where(lower, a, pltpu.roll(b, width, 1))
                chunks[i + bit] = jnp.where(lower, pltpu.roll(a, LANES - width, 1), b)
    return chunks


def runs_here(early):
    grp, lat, lon = (lax.axis_index(axis) for axis in ("grp", "lat", "lon"))
    held = jnp.logical_and(grp + lon == 0, lat < 3)
    first = jnp.logical_and(grp < lax.axis_size("grp") // 2, jnp.logical_not(held))
    return first if early else jnp.logical_not(first)


def local_kernel(early, *refs):
    inputs, outputs, scratch, sems = refs[:9], refs[-20:-16], refs[-16:-1], refs[-1]
    state_ref, low_ref, high_ref = inputs[6:]
    pre_ref, heat_ref, main_ref, send_ref = outputs

    @pl.when(runs_here(early))
    def _():
        copies = [pltpu.make_async_copy(inputs[i], scratch[9 + i], sems.at[i]) for i in range(6)]
        for copy in copies:
            copy.start()
        copies[5].wait()
        whole_step(scratch[14], state_ref, low_ref, high_ref, main_ref, send_ref, *scratch[:6], scratch[8])
        for copy in copies[:5]:
            copy.wait()
        chemistry(*scratch[9:14], pre_ref, heat_ref, *scratch[6:8])
        for y in range(4):
            send_ref[pl.ds(12 + y, PEERS, stride=SLOTS), :] = heat_ref[y]


def chemistry(rates_ref, pairs_ref, map_ref, coef_ref, q_ref, pre_ref, heat_ref, heat_sc, turn_sc):
    pre_ref[...] = q_ref[...]
    heat_sc[...] = jnp.zeros_like(heat_sc)

    def weight(species):
        return coef_ref[map_ref[species]]

    def react(r, carry):
        a, b, p = pairs_ref[0, r], pairs_ref[1, r], pairs_ref[2, r]
        rate = rates_ref[r] * q_ref[a] * q_ref[b]
        heat_sc[...] += (weight(p) - weight(a) - weight(b)) * rate
        pre_ref[p] += rate
        pre_ref[a] -= rate
        pre_ref[b] -= rate
        return carry

    lax.fori_loop(0, REACTIONS, react, 0)
    ordered = jnp.concatenate([heat_sc[pl.ds(y, ROWS, stride=4), :] for y in range(4)], 0)
    turn_sc[...] = jnp.transpose(ordered)
    chunks = [turn_sc[pl.ds(level, PEERS, stride=4), :] for level in range(4)]
    for y, block in enumerate(regroup(chunks)):
        heat_ref[y] = block


def lat_ends():
    lat = lax.axis_index("lat")
    return lat > 0, lat < lax.axis_size("lat") - 1


def whole_step(coupling_ref, state_ref, low_ref, high_ref, out_ref, send_ref, sa, sb, ta, tb, ua, ub, turn_sc):
    has_low, has_high = lat_ends()
    base = 16

    sb[...] = jnp.zeros_like(sb)
    for plane in range(PLANES):
        sa[plane, base - BAND : base, :] = low_ref[plane]
        sa[plane, base : base + ROWS, :] = state_ref[plane]
        sa[plane, base + ROWS : base + ROWS + BAND, :] = high_ref[plane]

    lane8 = lane_index(8)
    weights = [
        [coupling_ref[f, g] + (0.6 if f == g else 0.0) for g in range(FIELDS)] for f in range(FIELDS)
    ]

    def apply(a_ref, b_ref, z, row, both):
        centers_a = [a_ref[f * LEVELS + z, row : row + 8, :] for f in range(FIELDS)]
        centers_b = [b_ref[f * LEVELS + z, row : row + 8, :] for f in range(FIELDS)]

        def along_lanes(f):
            moved = {}
            for j in (1, 2, -1, -2):
                ra = pltpu.roll(centers_a[f], -j % LANES, 1)
                rb = pltpu.roll(centers_b[f], -j % LANES, 1)
                inner = lane8 < LANES - j if j > 0 else lane8 >= -j
                moved[j] = (jnp.where(inner, ra, rb), jnp.where(inner, rb, ra) if both else None)
            return moved

        result = []
        for f in range(FIELDS):
            moved = along_lanes(f)
            pieces = []
            for part, ref, centers in ((0, a_ref, centers_a), (1, b_ref, centers_b)):
                if part == 1 and not both:
                    break
                x = {j: ref[f * LEVELS + z, row + j : row + j + 8, :] for j in (1, 2, -1, -2)}
                total = -0.1 * (x[1] + moved[1][part]) + 0.3 * (x[-1] + moved[-1][part])
                total = total + 0.025 * ((x[2] - x[-2]) + (moved[2][part] - moved[-2][part]))
                for g in range(FIELDS):
                    total = total + weights[f][g] * centers[g]
                pieces.append(total)
            result.append(pieces)
        return result

    first, last = base - BAND, base + ROWS

    def masked(value, row):
        if row == first:
            return jnp.where(has_low, value, 0.0)
        if row == last:
            return jnp.where(has_high, value, 0.0)
        return value

    def stage_one(z, carry):
        for row in range(first, last + 8, 8):
            for f, (a, b) in enumerate(apply(sa, sb, z, row, True)):
                ta[f * LEVELS + z, row : row + 8, :] = masked(a, row)
                tb[f * LEVELS + z, row : row + 8, :] = masked(b, row)
        return carry

    def stage_two(z, carry):
        for row in range(first, last + 8, 8):
            for f, (a, b) in enumerate(apply(ta, tb, z, row, True)):
                plane = f * LEVELS + z
                ua[plane, row : row + 8, :] = masked(0.75 * sa[plane, row : row + 8, :] + 0.25 * a, row)
                ub[plane, row : row + 8, :] = masked(0.75 * sb[plane, row : row + 8, :] + 0.25 * b, row)
        return carry

    def stage_three(z, carry):
        for row in range(base, last, 8):
            for f, (a,) in enumerate(apply(ua, ub, z, row, False)):
                plane = f * LEVELS + z
                value = sa[plane, row : row + 8, :] * (1.0 / 3.0) + (2.0 / 3.0) * a
                out_ref[plane, row - base : row - base + 8, :] = value
        return carry

    lax.fori_loop(0, LEVELS, stage_one, 0)
    lax.fori_loop(0, LEVELS, stage_two, 0)
    lax.fori_loop(0, LEVELS, stage_three, 0)

    for f in range(3):
        plane = jnp.concatenate([out_ref[f * LEVELS + z] for z in range(LEVELS)], 0)
        turn_sc[f] = jnp.transpose(plane)
        chunks = [turn_sc[f, pl.ds(y, PEERS, stride=4), :] for y in range(4)]
        for level, block in enumerate(regroup(chunks)):
            send_ref[pl.ds(4 * f + level, PEERS, stride=SLOTS), :] = block


def edge_step_kernel(
    once_ref, twice_ref, main_ref, sent_ref, far_ref, near_ref, out_ref, send_ref, sa, sb, ta, tb, ua, ub, turn_sc
):
    odd = lax.rem(lax.axis_index("grp"), 2) == 1
    has_low, has_high = lat_ends()
    pad = 8
    zero = jnp.zeros((SPAN, LANES), jnp.float32)
    sa[pad : pad + SPAN, :] = jnp.where(odd, near_ref[...], far_ref[...])
    sa[pad + SPAN : pad + 2 * SPAN, :] = zero
    sb[pad : pad + SPAN, :] = zero
    sb[pad + SPAN : pad + 2 * SPAN, :] = jnp.where(odd, far_ref[...], near_ref[...])

    lanes = lane_index(8)
    column = lax.rem(lanes, HALO)
    field = lanes // (HALO * LEVELS)

    def mix_of(ref):
        mixes = {}
        for d in range(1 - FIELDS, FIELDS):
            total = jnp.zeros((8, LANES), jnp.float32)
            for f in range(max(d, 0), min(FIELDS, FIELDS + d)):
                total = jnp.where(field == f, ref[f, f - d], total)
            mixes[d] = total
        return mixes

    once, twice = mix_of(once_ref), mix_of(twice_ref)

    def turn(value, by):
        return pltpu.roll(value, by % LANES, 1) if by % LANES else value

    def apply(a_ref, b_ref, row, parts="ab"):
        a, b = a_ref[row : row + 8, :], b_ref[row : row + 8, :]
        out = []
        for part in parts:
            y = {}
            for j in (1, 2):
                inside, behind = column < HALO - j, column >= j
                if part == "a":
                    y[j] = jnp.where(inside, turn(a, -j), turn(b, HALO - j))
                    y[-j] = jnp.where(behind, turn(a, j), 0.0)
                else:
                    y[j] = jnp.where(inside, turn(b, -j), 0.0)
                    y[-j] = jnp.where(behind, turn(b, j), turn(a, j - HALO))
            ref = a_ref if part == "a" else b_ref
            x = {j: ref[row + j : row + j + 8, :] for j in (1, 2, -1, -2)}
            total = -0.1 * (x[1] + y[1]) + 0.3 * (x[-1] + y[-1])
            total = total + 0.025 * ((x[2] - x[-2]) + (y[2] - y[-2]))
            out.append(total - 0.4 * (a if part == "a" else b))
        return out

    def mixed(mixes, value):
        total = None
        for d, mix in mixes.items():
            term = mix * turn(value, HALO * LEVELS * d)
            total = term if total is None else total + term
        return total

    def masked(value, row):
        place = (row - pad) % SPAN
        if place < BAND:
            return jnp.where(has_low, value, 0.0)
        if place >= BAND + ROWS:
            return jnp.where(has_high, value, 0.0)
        return value

    every = range(pad, pad + 2 * SPAN, 8)
    for row in every:
        a, b = apply(sa, sb, row)
        ta[row : row + 8, :] = masked(a, row)
        tb[row : row + 8, :] = masked(b, row)
    for row in every:
        a, b = apply(ta, tb, row)
        ua[row : row + 8, :] = masked(a, row)
        ub[row : row + 8, :] = masked(b, row)
    firsts, finals = [], []
    for row in range(pad + BAND, pad + BAND + ROWS, 8):
        (b,) = apply(ua, ub, row, "b")
        (a,) = apply(ua, ub, row + SPAN, "a")
        first = mixed(twice, tb[row : row + 8, :]) + mixed(once, 0.5 * ub[row : row + 8, :]) + b * (1.0 / 6.0)
        other = row + SPAN
        final = mixed(twice, ta[other : other + 8, :]) + mixed(once, 0.5 * ua[other : other + 8, :]) + a * (1.0 / 6.0)
        firsts.append(first)
        finals.append(final)
        place = row - pad - BAND
        for plane in range(PLANES):
            gain = jnp.where(lanes < HALO, turn(first, -HALO * plane), 0.0)
            gain = jnp.where(lanes >= LANES - HALO, turn(final, LANES - HALO - HALO * plane), gain)
            out_ref[plane, place : place + 8, :] = main_ref[plane, place : place + 8, :] + gain

    winds = 3 * LEVELS
    lanes12 = lane_index(winds)
    zeros = jnp.zeros((LANES - ROWS, LANES), jnp.float32)
    for side, values in ((0, firsts), (1, finals)):
        turn_sc[side] = jnp.transpose(jnp.concatenate(values + [zeros], 0))
        for peer in (0, 1) if side == 0 else (PEERS - 2, PEERS - 1):
            gain = jnp.zeros((winds, LANES), jnp.float32)
            for y in range(4):
                c = 4 * peer + y - (LANES - HALO if side else 0)
                if 0 <= c < HALO:
                    part = turn_sc[side, pl.ds(c, winds, stride=HALO), :]
                    here = jnp.logical_and(lanes12 >= ROWS * y, lanes12 < ROWS * y + ROWS)
                    gain = jnp.where(here, turn(part, ROWS * y), gain)
            send_ref[peer * SLOTS : peer * SLOTS + winds, :] += gain


def final_kernel(recv_ref, stepped_ref, q_ref, pre_ref, state_out_ref, q_out_ref, turn_sc, wind_sc, temp_sc, q_sc, sems):
    copies = []

    def send_out(source, target):
        copy = pltpu.make_async_copy(source, target, sems.at[len(copies)])
        copy.start()
        copies.append(copy)

    send_out(stepped_ref.at[0:3], state_out_ref.at[0:3])
    send_out(stepped_ref.at[4:5], state_out_ref.at[4:5])
    for f in range(3):
        for level in range(4):
            turn_sc[pl.ds(level, PEERS, stride=4), :] = recv_ref[pl.ds(4 * f + level, PEERS, stride=SLOTS), :]
        columns = jnp.transpose(turn_sc[...])
        for y in range(4):
            wind_sc[f, pl.ds(y, ROWS, stride=4), :] = columns[y * ROWS : (y + 1) * ROWS]

    chunk = 32
    lanes = lane_index(chunk)

    def clamped(value):
        higher = jnp.where(lanes == LANES - 1, value, pltpu.roll(value, LANES - 1, 1))
        lower = jnp.where(lanes == 0, value, pltpu.roll(value, 1, 1))
        return higher, lower

    for start in range(0, 128, chunk):
        rows = slice(start, start + chunk)
        shear = None
        for f in range(2):
            higher, lower = clamped(wind_sc[f, rows, :])
            square = (higher - lower) * (higher - lower)
            shear = square if shear is None else shear + square
        mixing = 0.2 * shear / (1.0 + shear)
        vertical = wind_sc[2, rows, :]
        speed = 0.4 * vertical / (1.0 + jnp.abs(vertical))
        up = mixing - jnp.minimum(speed, 0.0)
        down = mixing + jnp.maximum(speed, 0.0)
        for s in range(SPECIES):
            value = q_ref[s, rows, :]
            higher, lower = clamped(value)
            q_sc[s, rows, :] = pre_ref[s, rows, :] + (up * (higher - value) - down * (value - lower))
        send_out(q_sc.at[:, rows, :], q_out_ref.at[:, rows, :])
        if start == 0:
            for y in range(4):
                turn_sc[pl.ds(y, PEERS, stride=4), :] = recv_ref[pl.ds(12 + y, PEERS, stride=SLOTS), :]
            temp_sc[0] = stepped_ref[3] + 0.5 * jnp.transpose(turn_sc[...])
            send_out(temp_sc, state_out_ref.at[3:4])
    for copy in copies:
        copy.wait()


VMEM = pl.BlockSpec(memory_space=pltpu.VMEM)
SMEM = pl.BlockSpec(memory_space=pltpu.SMEM)
PARAMS = pltpu.CompilerParams(vmem_limit_bytes=16 * 1024 * 1024)


def shape(*dims):
    return jax.ShapeDtypeStruct(dims, jnp.float32)


def cost(flops, data):
    return pl.CostEstimate(flops=flops, bytes_accessed=data, transcendentals=0)


def on_device(state, tracers, coupling, rates, pairs, heat_map, heat_coef):
    planes = state.reshape(PLANES, ROWS, LANES)
    outside = pl.BlockSpec(memory_space=pltpu.HBM)
    q = tracers.reshape(SPECIES, 128, 128)

    count = lax.axis_size("lat")
    low = lax.ppermute(planes[:, ROWS - BAND :], "lat", [(i, i + 1) for i in range(count - 1)])
    high = lax.ppermute(planes[:, :BAND], "lat", [(i + 1, i) for i in range(count - 1)])
    once = jnp.eye(FIELDS, dtype=jnp.float32) + coupling
    squared = jnp.sum(coupling[:, :, None] * coupling[None, :, :], 1)
    twice = once + 0.5 * squared
    reactants = (rates, pairs.T, heat_map, heat_coef, q)

    own_far, own_near = pl.pallas_call(
        own_kernel,
        out_shape=(shape(ROWS, LANES),) * 2,
        in_specs=[VMEM],
        out_specs=(VMEM,) * 2,
        cost_estimate=cost(1000000, 400000),
        compiler_params=PARAMS,
    )(planes)
    extended = pltpu.VMEM((PLANES, 64, LANES), jnp.float32)
    square = pltpu.VMEM((128, 128), jnp.float32)

    def local(early, *before):
        return pl.pallas_call(
            functools.partial(local_kernel, early),
            out_shape=(
                shape(SPECIES, 128, 128),
                shape(4, PEERS, LANES),
                shape(PLANES, ROWS, LANES),
                shape(PEERS * SLOTS, LANES),
            ),
            in_specs=[outside] * 6 + [VMEM] * (3 + len(before)),
            out_specs=(VMEM,) * 4,
            scratch_shapes=[extended] * 6
            + [square] * 2
            + [pltpu.VMEM((3, 128, 128), jnp.float32)]
            + [pltpu.SMEM(rates.shape, jnp.float32), pltpu.SMEM((3, REACTIONS), jnp.int32)]
            + [pltpu.SMEM(heat_map.shape, jnp.int32), pltpu.SMEM(heat_coef.shape, jnp.float32)]
            + [pltpu.VMEM((SPECIES, 128, 128), jnp.float32), pltpu.SMEM(coupling.shape, jnp.float32)]
            + [pltpu.SemaphoreType.DMA((6,))],
            input_output_aliases={9 + i: i for i in range(len(before))},
            cost_estimate=cost(30000000, 3000000),
            compiler_params=PARAMS,
        )(*(pltpu.with_memory_space_constraint(x, pltpu.HBM) for x in (*reactants, coupling)), planes, low, high, *before)

    done = local(True)
    low, high, once, twice, *done = lax.optimization_barrier((low, high, once, twice, *done))
    far, near = pl.pallas_call(
        pack_kernel,
        out_shape=(shape(SPAN, LANES), shape(SPAN, LANES)),
        in_specs=[VMEM] * 4,
        out_specs=(VMEM, VMEM),
        cost_estimate=cost(1000000, 400000),
        compiler_params=PARAMS,
    )(low, high, own_far, own_near)
    far, near, low, high, *done = lax.optimization_barrier((far, near, low, high, *done))
    far_in = lax.ppermute(far, "grp", [(0, 3), (3, 0), (1, 2), (2, 1)])
    near_in = lax.ppermute(near, "grp", [(0, 1), (1, 0), (2, 3), (3, 2)])
    pre, _, main, sent = local(False, *done)
    window = pltpu.VMEM((2 * SPAN + 16, LANES), jnp.float32)
    stepped, send = pl.pallas_call(
        edge_step_kernel,
        out_shape=(shape(PLANES, ROWS, LANES), shape(PEERS * SLOTS, LANES)),
        in_specs=[SMEM] * 2 + [VMEM] * 4,
        out_specs=(VMEM, VMEM),
        scratch_shapes=[window] * 6 + [pltpu.VMEM((2, 128, 128), jnp.float32)],
        input_output_aliases={3: 1},
        cost_estimate=cost(2000000, 1000000),
        compiler_params=PARAMS,
    )(once, twice, main, sent, far_in, near_in)

    received = lax.all_to_all(
        send.reshape(PEERS, SLOTS, LANES), "lon", split_axis=0, concat_axis=0, tiled=True
    )
    state_out, q_out = pl.pallas_call(
        final_kernel,
        out_shape=(shape(FIELDS, 128, 128), shape(SPECIES, 128, 128)),
        in_specs=[VMEM] * 4,
        out_specs=(outside,) * 2,
        scratch_shapes=[
            square,
            pltpu.VMEM((3, 128, 128), jnp.float32),
            pltpu.VMEM((1, 128, 128), jnp.float32),
            pltpu.VMEM((SPECIES, 128, 128), jnp.float32),
            pltpu.SemaphoreType.DMA((7,)),
        ],
        cost_estimate=cost(10000000, 2500000),
        compiler_params=PARAMS,
    )(received.reshape(PEERS * SLOTS, LANES), stepped.reshape(FIELDS, 128, 128), q, pre)
    return state_out.reshape(state.shape), q_out.reshape(tracers.shape)


def solution(mesh):
    in_specs = (
        P(None, "lon", "lat", "grp"),
        P(None, "lat", ("grp", "lon"), None),
        P(),
        P(),
        P(),
        P(),
        P(),
    )
    out_specs = (P(None, "lon", "lat", "grp"), P(None, "lat", ("grp", "lon"), None))
    return jax.shard_map(
        on_device, mesh=mesh, in_specs=in_specs, out_specs=out_specs, check_vma=False
    )
```

```python
import functools

import jax
import jax.numpy as jnp
from jax import lax
from jax.experimental import pallas as pl
from jax.experimental.pallas import tpu as pltpu
from jax.sharding import PartitionSpec as P


FIELDS = 5
LEVELS = 4
PLANES = FIELDS * LEVELS
ROWS = 32
LANES = 128
HALO = 6
BAND = 8
SPAN = ROWS + 2 * BAND
PEERS = 32
SLOTS = 16
SPECIES = 12
REACTIONS = 24


def lane_index(rows):
    return lax.broadcasted_iota(jnp.int32, (rows, LANES), 1)


def packed(tiles):
    lanes = lane_index(tiles[0].shape[0])
    left = tiles[0]
    right = pltpu.roll(tiles[0], HALO, 1)
    for plane in range(1, PLANES):
        keep = lanes >= HALO * plane
        left = jnp.where(keep, pltpu.roll(tiles[plane], HALO * plane, 1), left)
        right = jnp.where(keep, pltpu.roll(tiles[plane], (HALO * plane + HALO) % LANES, 1), right)
    odd = lax.rem(lax.axis_index("grp"), 2) == 1
    return jnp.where(odd, right, left), jnp.where(odd, left, right)


def own_kernel(state_ref, far_ref, near_ref):
    far_ref[...], near_ref[...] = packed([state_ref[plane] for plane in range(PLANES)])


def pack_kernel(low_ref, high_ref, own_far_ref, own_near_ref, far_ref, near_ref):
    far_ref[BAND : BAND + ROWS] = own_far_ref[...]
    near_ref[BAND : BAND + ROWS] = own_near_ref[...]
    unused = jnp.zeros((BAND - HALO, LANES), jnp.float32)
    low = [low_ref[HALO * plane : HALO * plane + HALO] for plane in range(PLANES)]
    high = [high_ref[HALO * plane : HALO * plane + HALO] for plane in range(PLANES)]
    for ref, under, over in zip((far_ref, near_ref), packed(low), packed(high), strict=True):
        ref[:BAND] = jnp.concatenate([unused, under], 0)
        ref[BAND + ROWS :] = jnp.concatenate([over, unused], 0)


def regroup(chunks):
    lanes = lane_index(ROWS)
    chunks = list(chunks)
    for bit in (2, 1):
        width = bit * LANES // 4
        lower = lax.rem(lanes // width, 2) == 0
        for i in range(4):
            if not i & bit:
                a, b = chunks[i], chunks[i + bit]
                chunks[i] = jnp.where(lower, a, pltpu.roll(b, width, 1))
                chunks[i + bit] = jnp.where(lower, pltpu.roll(a, LANES - width, 1), b)
    return chunks


def runs_here(early):
    grp, lat, lon = (lax.axis_index(axis) for axis in ("grp", "lat", "lon"))
    held = jnp.logical_and(grp + lon == 0, lat < 3)
    first = jnp.logical_and(grp < lax.axis_size("grp") // 2, jnp.logical_not(held))
    return first if early else jnp.logical_not(first)


def local_kernel(early, *refs):
    inputs, outputs, scratch, sems = refs[:9], refs[-20:-16], refs[-16:-1], refs[-1]
    state_ref, low_ref, high_ref = inputs[6:]
    pre_ref, heat_ref, main_ref, send_ref = outputs

    @pl.when(runs_here(early))
    def _():
        copies = [pltpu.make_async_copy(inputs[i], scratch[9 + i], sems.at[i]) for i in range(6)]
        for copy in copies:
            copy.start()
        copies[5].wait()
        whole_step(scratch[14], state_ref, low_ref, high_ref, main_ref, send_ref, *scratch[:6], scratch[8])
        for copy in copies[:5]:
            copy.wait()
        chemistry(*scratch[9:14], pre_ref, heat_ref, *scratch[6:8])
        for y in range(4):
            send_ref[pl.ds(12 + y, PEERS, stride=SLOTS), :] = heat_ref[y]


def chemistry(rates_ref, pairs_ref, map_ref, coef_ref, q_ref, pre_ref, heat_ref, heat_sc, turn_sc):
    pre_ref[...] = q_ref[...]
    heat_sc[...] = jnp.zeros_like(heat_sc)

    def weight(species):
        return coef_ref[map_ref[species]]

    def react(r, carry):
        a, b, p = pairs_ref[0, r], pairs_ref[1, r], pairs_ref[2, r]
        rate = rates_ref[r] * q_ref[a] * q_ref[b]
        heat_sc[...] += (weight(p) - weight(a) - weight(b)) * rate
        pre_ref[p] += rate
        pre_ref[a] -= rate
        pre_ref[b] -= rate
        return carry

    lax.fori_loop(0, REACTIONS, react, 0)
    ordered = jnp.concatenate([heat_sc[pl.ds(y, ROWS, stride=4), :] for y in range(4)], 0)
    turn_sc[...] = jnp.transpose(ordered)
    chunks = [turn_sc[pl.ds(level, PEERS, stride=4), :] for level in range(4)]
    for y, block in enumerate(regroup(chunks)):
        heat_ref[y] = block


def lat_ends():
    lat = lax.axis_index("lat")
    return lat > 0, lat < lax.axis_size("lat") - 1


def whole_step(coupling_ref, state_ref, low_ref, high_ref, out_ref, send_ref, sa, sb, ta, tb, ua, ub, turn_sc):
    has_low, has_high = lat_ends()
    base = 16

    sb[...] = jnp.zeros_like(sb)
    for plane in range(PLANES):
        sa[plane, base - HALO : base, :] = low_ref[HALO * plane : HALO * plane + HALO]
        sa[plane, base : base + ROWS, :] = state_ref[plane]
        sa[plane, base + ROWS : base + ROWS + HALO, :] = high_ref[HALO * plane : HALO * plane + HALO]

    lane8 = lane_index(8)
    weights = [
        [coupling_ref[f, g] + (0.6 if f == g else 0.0) for g in range(FIELDS)] for f in range(FIELDS)
    ]

    def apply(a_ref, b_ref, z, row, both):
        centers_a = [a_ref[f * LEVELS + z, row : row + 8, :] for f in range(FIELDS)]
        centers_b = [b_ref[f * LEVELS + z, row : row + 8, :] for f in range(FIELDS)]

        def along_lanes(f):
            moved = {}
            for j in (1, 2, -1, -2):
                ra = pltpu.roll(centers_a[f], -j % LANES, 1)
                rb = pltpu.roll(centers_b[f], -j % LANES, 1)
                inner = lane8 < LANES - j if j > 0 else lane8 >= -j
                moved[j] = (jnp.where(inner, ra, rb), jnp.where(inner, rb, ra) if both else None)
            return moved

        result = []
        for f in range(FIELDS):
            moved = along_lanes(f)
            pieces = []
            for part, ref, centers in ((0, a_ref, centers_a), (1, b_ref, centers_b)):
                if part == 1 and not both:
                    break
                x = {j: ref[f * LEVELS + z, row + j : row + j + 8, :] for j in (1, 2, -1, -2)}
                total = -0.1 * (x[1] + moved[1][part]) + 0.3 * (x[-1] + moved[-1][part])
                total = total + 0.025 * ((x[2] - x[-2]) + (moved[2][part] - moved[-2][part]))
                for g in range(FIELDS):
                    total = total + weights[f][g] * centers[g]
                pieces.append(total)
            result.append(pieces)
        return result

    first, last = base - BAND, base + ROWS

    def masked(value, row):
        if row == first:
            return jnp.where(has_low, value, 0.0)
        if row == last:
            return jnp.where(has_high, value, 0.0)
        return value

    def stage_one(z, carry):
        for row in range(first, last + 8, 8):
            for f, (a, b) in enumerate(apply(sa, sb, z, row, True)):
                ta[f * LEVELS + z, row : row + 8, :] = masked(a, row)
                tb[f * LEVELS + z, row : row + 8, :] = masked(b, row)
        return carry

    def stage_two(z, carry):
        for row in range(first, last + 8, 8):
            for f, (a, b) in enumerate(apply(ta, tb, z, row, True)):
                plane = f * LEVELS + z
                ua[plane, row : row + 8, :] = masked(0.75 * sa[plane, row : row + 8, :] + 0.25 * a, row)
                ub[plane, row : row + 8, :] = masked(0.75 * sb[plane, row : row + 8, :] + 0.25 * b, row)
        return carry

    def stage_three(z, carry):
        for row in range(base, last, 8):
            for f, (a,) in enumerate(apply(ua, ub, z, row, False)):
                plane = f * LEVELS + z
                value = sa[plane, row : row + 8, :] * (1.0 / 3.0) + (2.0 / 3.0) * a
                out_ref[plane, row - base : row - base + 8, :] = value
        return carry

    lax.fori_loop(0, LEVELS, stage_one, 0)
    lax.fori_loop(0, LEVELS, stage_two, 0)
    lax.fori_loop(0, LEVELS, stage_three, 0)

    for f in range(3):
        plane = jnp.concatenate([out_ref[f * LEVELS + z] for z in range(LEVELS)], 0)
        turn_sc[f] = jnp.transpose(plane)
        chunks = [turn_sc[f, pl.ds(y, PEERS, stride=4), :] for y in range(4)]
        for level, block in enumerate(regroup(chunks)):
            send_ref[pl.ds(4 * f + level, PEERS, stride=SLOTS), :] = block


def edge_step_kernel(
    once_ref, twice_ref, main_ref, sent_ref, far_ref, near_ref, out_ref, send_ref, sa, sb, ta, tb, ua, ub, turn_sc
):
    odd = lax.rem(lax.axis_index("grp"), 2) == 1
    has_low, has_high = lat_ends()
    pad = 8
    zero = jnp.zeros((SPAN, LANES), jnp.float32)
    sa[pad : pad + SPAN, :] = jnp.where(odd, near_ref[...], far_ref[...])
    sa[pad + SPAN : pad + 2 * SPAN, :] = zero
    sb[pad : pad + SPAN, :] = zero
    sb[pad + SPAN : pad + 2 * SPAN, :] = jnp.where(odd, far_ref[...], near_ref[...])

    lanes = lane_index(8)
    column = lax.rem(lanes, HALO)
    field = lanes // (HALO * LEVELS)

    def mix_of(ref):
        mixes = {}
        for d in range(1 - FIELDS, FIELDS):
            total = jnp.zeros((8, LANES), jnp.float32)
            for f in range(max(d, 0), min(FIELDS, FIELDS + d)):
                total = jnp.where(field == f, ref[f, f - d], total)
            mixes[d] = total
        return mixes

    once, twice = mix_of(once_ref), mix_of(twice_ref)

    def turn(value, by):
        return pltpu.roll(value, by % LANES, 1) if by % LANES else value

    def apply(a_ref, b_ref, row, parts="ab"):
        a, b = a_ref[row : row + 8, :], b_ref[row : row + 8, :]
        out = []
        for part in parts:
            y = {}
            for j in (1, 2):
                inside, behind = column < HALO - j, column >= j
                if part == "a":
                    y[j] = jnp.where(inside, turn(a, -j), turn(b, HALO - j))
                    y[-j] = jnp.where(behind, turn(a, j), 0.0)
                else:
                    y[j] = jnp.where(inside, turn(b, -j), 0.0)
                    y[-j] = jnp.where(behind, turn(b, j), turn(a, j - HALO))
            ref = a_ref if part == "a" else b_ref
            x = {j: ref[row + j : row + j + 8, :] for j in (1, 2, -1, -2)}
            total = -0.1 * (x[1] + y[1]) + 0.3 * (x[-1] + y[-1])
            total = total + 0.025 * ((x[2] - x[-2]) + (y[2] - y[-2]))
            out.append(total - 0.4 * (a if part == "a" else b))
        return out

    def mixed(mixes, value):
        total = None
        for d, mix in mixes.items():
            term = mix * turn(value, HALO * LEVELS * d)
            total = term if total is None else total + term
        return total

    def masked(value, row):
        place = (row - pad) % SPAN
        if place < BAND:
            return jnp.where(has_low, value, 0.0)
        if place >= BAND + ROWS:
            return jnp.where(has_high, value, 0.0)
        return value

    every = range(pad, pad + 2 * SPAN, 8)
    for row in every:
        a, b = apply(sa, sb, row)
        ta[row : row + 8, :] = masked(a, row)
        tb[row : row + 8, :] = masked(b, row)
    for row in every:
        a, b = apply(ta, tb, row)
        ua[row : row + 8, :] = masked(a, row)
        ub[row : row + 8, :] = masked(b, row)
    firsts, finals = [], []
    for row in range(pad + BAND, pad + BAND + ROWS, 8):
        (b,) = apply(ua, ub, row, "b")
        (a,) = apply(ua, ub, row + SPAN, "a")
        first = mixed(twice, tb[row : row + 8, :]) + mixed(once, 0.5 * ub[row : row + 8, :]) + b * (1.0 / 6.0)
        other = row + SPAN
        final = mixed(twice, ta[other : other + 8, :]) + mixed(once, 0.5 * ua[other : other + 8, :]) + a * (1.0 / 6.0)
        firsts.append(first)
        finals.append(final)
        place = row - pad - BAND
        for plane in range(PLANES):
            gain = jnp.where(lanes < HALO, turn(first, -HALO * plane), 0.0)
            gain = jnp.where(lanes >= LANES - HALO, turn(final, LANES - HALO - HALO * plane), gain)
            out_ref[plane, place : place + 8, :] = main_ref[plane, place : place + 8, :] + gain

    winds = 3 * LEVELS
    lanes12 = lane_index(winds)
    zeros = jnp.zeros((LANES - ROWS, LANES), jnp.float32)
    for side, values in ((0, firsts), (1, finals)):
        turn_sc[side] = jnp.transpose(jnp.concatenate(values + [zeros], 0))
        for peer in (0, 1) if side == 0 else (PEERS - 2, PEERS - 1):
            gain = jnp.zeros((winds, LANES), jnp.float32)
            for y in range(4):
                c = 4 * peer + y - (LANES - HALO if side else 0)
                if 0 <= c < HALO:
                    part = turn_sc[side, pl.ds(c, winds, stride=HALO), :]
                    here = jnp.logical_and(lanes12 >= ROWS * y, lanes12 < ROWS * y + ROWS)
                    gain = jnp.where(here, turn(part, ROWS * y), gain)
            send_ref[peer * SLOTS : peer * SLOTS + winds, :] += gain


def final_kernel(recv_ref, stepped_ref, q_ref, pre_ref, state_out_ref, q_out_ref, turn_sc, wind_sc, temp_sc, q_sc, sems):
    copies = []

    def send_out(source, target):
        copy = pltpu.make_async_copy(source, target, sems.at[len(copies)])
        copy.start()
        copies.append(copy)

    send_out(stepped_ref.at[0:3], state_out_ref.at[0:3])
    send_out(stepped_ref.at[4:5], state_out_ref.at[4:5])
    for f in range(3):
        for level in range(4):
            turn_sc[pl.ds(level, PEERS, stride=4), :] = recv_ref[pl.ds(4 * f + level, PEERS, stride=SLOTS), :]
        columns = jnp.transpose(turn_sc[...])
        for y in range(4):
            wind_sc[f, pl.ds(y, ROWS, stride=4), :] = columns[y * ROWS : (y + 1) * ROWS]

    chunk = 32
    lanes = lane_index(chunk)

    def clamped(value):
        higher = jnp.where(lanes == LANES - 1, value, pltpu.roll(value, LANES - 1, 1))
        lower = jnp.where(lanes == 0, value, pltpu.roll(value, 1, 1))
        return higher, lower

    for start in range(0, 128, chunk):
        rows = slice(start, start + chunk)
        shear = None
        for f in range(2):
            higher, lower = clamped(wind_sc[f, rows, :])
            square = (higher - lower) * (higher - lower)
            shear = square if shear is None else shear + square
        mixing = 0.2 * shear / (1.0 + shear)
        vertical = wind_sc[2, rows, :]
        speed = 0.4 * vertical / (1.0 + jnp.abs(vertical))
        up = mixing - jnp.minimum(speed, 0.0)
        down = mixing + jnp.maximum(speed, 0.0)
        for s in range(SPECIES):
            value = q_ref[s, rows, :]
            higher, lower = clamped(value)
            q_sc[s, rows, :] = pre_ref[s, rows, :] + (up * (higher - value) - down * (value - lower))
        send_out(q_sc.at[:, rows, :], q_out_ref.at[:, rows, :])
        if start == 0:
            for y in range(4):
                turn_sc[pl.ds(y, PEERS, stride=4), :] = recv_ref[pl.ds(12 + y, PEERS, stride=SLOTS), :]
            temp_sc[0] = stepped_ref[3] + 0.5 * jnp.transpose(turn_sc[...])
            send_out(temp_sc, state_out_ref.at[3:4])
    for copy in copies:
        copy.wait()


VMEM = pl.BlockSpec(memory_space=pltpu.VMEM)
SMEM = pl.BlockSpec(memory_space=pltpu.SMEM)
PARAMS = pltpu.CompilerParams(vmem_limit_bytes=16 * 1024 * 1024)


def shape(*dims):
    return jax.ShapeDtypeStruct(dims, jnp.float32)


def cost(flops, data):
    return pl.CostEstimate(flops=flops, bytes_accessed=data, transcendentals=0)


def on_device(state, tracers, coupling, rates, pairs, heat_map, heat_coef):
    planes = state.reshape(PLANES, ROWS, LANES)
    outside = pl.BlockSpec(memory_space=pltpu.HBM)
    q = tracers.reshape(SPECIES, 128, 128)

    count = lax.axis_size("lat")
    high = lax.ppermute(planes[:, :HALO].reshape(PLANES * HALO, LANES), "lat", [(i + 1, i) for i in range(count - 1)])
    low = lax.ppermute(planes[:, ROWS - HALO :].reshape(PLANES * HALO, LANES), "lat", [(i, i + 1) for i in range(count - 1)])
    once = jnp.eye(FIELDS, dtype=jnp.float32) + coupling
    squared = jnp.sum(coupling[:, :, None] * coupling[None, :, :], 1)
    twice = once + 0.5 * squared
    reactants = (rates, pairs.T, heat_map, heat_coef, q)

    own_far, own_near = pl.pallas_call(
        own_kernel,
        out_shape=(shape(ROWS, LANES),) * 2,
        in_specs=[VMEM],
        out_specs=(VMEM,) * 2,
        cost_estimate=cost(1000000, 400000),
        compiler_params=PARAMS,
    )(planes)
    extended = pltpu.VMEM((PLANES, 64, LANES), jnp.float32)
    square = pltpu.VMEM((128, 128), jnp.float32)

    def local(early, *before):
        return pl.pallas_call(
            functools.partial(local_kernel, early),
            out_shape=(
                shape(SPECIES, 128, 128),
                shape(4, PEERS, LANES),
                shape(PLANES, ROWS, LANES),
                shape(PEERS * SLOTS, LANES),
            ),
            in_specs=[outside] * 6 + [VMEM] * (3 + len(before)),
            out_specs=(VMEM,) * 4,
            scratch_shapes=[extended] * 6
            + [square] * 2
            + [pltpu.VMEM((3, 128, 128), jnp.float32)]
            + [pltpu.SMEM(rates.shape, jnp.float32), pltpu.SMEM((3, REACTIONS), jnp.int32)]
            + [pltpu.SMEM(heat_map.shape, jnp.int32), pltpu.SMEM(heat_coef.shape, jnp.float32)]
            + [pltpu.VMEM((SPECIES, 128, 128), jnp.float32), pltpu.SMEM(coupling.shape, jnp.float32)]
            + [pltpu.SemaphoreType.DMA((6,))],
            input_output_aliases={9 + i: i for i in range(len(before))},
            cost_estimate=cost(30000000, 3000000),
            compiler_params=PARAMS,
        )(*(pltpu.with_memory_space_constraint(x, pltpu.HBM) for x in (*reactants, coupling)), planes, low, high, *before)

    done = local(True)
    low, high, once, twice, *done = lax.optimization_barrier((low, high, once, twice, *done))
    far, near = pl.pallas_call(
        pack_kernel,
        out_shape=(shape(SPAN, LANES), shape(SPAN, LANES)),
        in_specs=[VMEM] * 4,
        out_specs=(VMEM, VMEM),
        cost_estimate=cost(1000000, 400000),
        compiler_params=PARAMS,
    )(low, high, own_far, own_near)
    far, near, low, high, *done = lax.optimization_barrier((far, near, low, high, *done))
    far_in = lax.ppermute(far, "grp", [(0, 3), (3, 0), (1, 2), (2, 1)])
    near_in = lax.ppermute(near, "grp", [(0, 1), (1, 0), (2, 3), (3, 2)])
    pre, _, main, sent = local(False, *done)
    window = pltpu.VMEM((2 * SPAN + 16, LANES), jnp.float32)
    stepped, send = pl.pallas_call(
        edge_step_kernel,
        out_shape=(shape(PLANES, ROWS, LANES), shape(PEERS * SLOTS, LANES)),
        in_specs=[SMEM] * 2 + [VMEM] * 4,
        out_specs=(VMEM, VMEM),
        scratch_shapes=[window] * 6 + [pltpu.VMEM((2, 128, 128), jnp.float32)],
        input_output_aliases={3: 1},
        cost_estimate=cost(2000000, 1000000),
        compiler_params=PARAMS,
    )(once, twice, main, sent, far_in, near_in)

    received = lax.all_to_all(
        send.reshape(PEERS, SLOTS, LANES), "lon", split_axis=0, concat_axis=0, tiled=True
    )
    state_out, q_out = pl.pallas_call(
        final_kernel,
        out_shape=(shape(FIELDS, 128, 128), shape(SPECIES, 128, 128)),
        in_specs=[VMEM] * 4,
        out_specs=(outside,) * 2,
        scratch_shapes=[
            square,
            pltpu.VMEM((3, 128, 128), jnp.float32),
            pltpu.VMEM((1, 128, 128), jnp.float32),
            pltpu.VMEM((SPECIES, 128, 128), jnp.float32),
            pltpu.SemaphoreType.DMA((7,)),
        ],
        cost_estimate=cost(10000000, 2500000),
        compiler_params=PARAMS,
    )(received.reshape(PEERS * SLOTS, LANES), stepped.reshape(FIELDS, 128, 128), q, pre)
    return state_out.reshape(state.shape), q_out.reshape(tracers.shape)


def solution(mesh):
    in_specs = (
        P(None, "lon", "lat", "grp"),
        P(None, "lat", ("grp", "lon"), None),
        P(),
        P(),
        P(),
        P(),
        P(),
    )
    out_specs = (P(None, "lon", "lat", "grp"), P(None, "lat", ("grp", "lon"), None))
    return jax.shard_map(on_device, mesh=mesh, in_specs=in_specs, out_specs=out_specs, check_vma=False)
```
